256 devices in a mesh: grp: 2 (over core), dev: 128 (over z, x, y).
Axes of the slice: x: 4, y: 4, z: 8, core: 2. Of those that a mesh axis runs over, the one named last changes fastest.
Arguments:
- disp: float32 [3, 512], P(None, 'dev'), may hold values from -6 to 6
- probe: float32 [3, 512], P(None, 'dev'), may hold values from -6 to 6
- strain_disp: float32 [6, 24, 256], P(None, None, 'dev'), may hold values from -1.25 to 1.25
- conn: int32 [8, 256], P(None, 'dev'), may hold values from 0 to 5
- halo_rows: int32 [256], P('dev'), may hold values from 0 to 3
- owner: int32 [256, 1], replicated, may hold values from 0 to 127; in each aligned block of 256 rows (0 to 255, 256 to 511, ...) at most 3 rows name the same one
- counts: int32 [256], replicated, may hold values from 1 to 2
- phase: int32 [128, 32768], P('dev'), may hold values 0 or 1
Outputs:
- point_stress: float32 [6, 256], P(None, 'dev')
- internal_force: float32 [3, 512], P(None, 'dev')
- stiffness_image: float32 [3, 512], P(None, 'dev')
The draws below stay inside these ranges and needn't reach their ends.
Inputs may be any that keep to these rules, and one draw needn't show every extreme that they name: Each owner has at most 3 points, and some owner has exactly 3. `conn`: local node numbers: the partition's 4 nodes, then 1 nodes received from the partition below, then 1 from the partition above.
All inputs are finite; a program needn't handle non-finite values. No bound on the sum of `phase` on one device may be relied on, other than what follows from the above.
Results may differ from the reference program's by a relative error of at most 0.0003.
Values sent between devices are 32-bit elements; how exact they have to be, the bound alone decides.
A program may use at most 64 MiB of HBM per device.

```python
import math
import jax
import jax.numpy as jnp
import numpy as np
from jax import lax

NV = 32
VOX = 32768
PT_DEV = 2
ITER_HI = 2
POINTS = 256
NODE_DEV = 4
HALO = 1
OWN_MAX = 3
N_DEV = 128


def with_ends(drawn, stream_key, least, top_value):
    longest = drawn.shape.index(max(drawn.shape))
    spots = []
    for shift in (0, 1):
        where = [jax.random.randint(jax.random.fold_in(stream_key, axis), (), 0, length) for axis, length in enumerate(drawn.shape)]
        where[longest] = (where[longest] + shift) % drawn.shape[longest]
        spots.append(tuple(where))
    return drawn.at[spots[0]].set(least).at[spots[1]].set(top_value)


def block_levels(stream_key, shape, shards, smallest, largest):
    def one(dim, shards_of):
        heights = jax.random.uniform(jax.random.fold_in(jax.random.fold_in(stream_key, 6), dim), (shards_of,), jnp.float32, smallest / len(shards), largest / len(shards))
        return jnp.repeat(jnp.exp(heights), shape[dim] // shards_of).reshape((-1,) + (1,) * (len(shape) - dim - 1))

    loudness = one(*shards[0])
    for cut in shards[1:]:
        loudness = loudness * one(*cut)
    return loudness


def shared_out(own_key, own, number, rows, number_of, top, limit, skew):
    order = jax.random.permutation(own_key, number_of)
    packed, usual = portions_of(number_of, rows * top, limit, skew, True), portions_of(number_of, rows * top, limit, skew, False)
    places = jnp.arange(number_of)

    def named(sizes, offset_by):
        used = int((sizes > 0).sum())
        fixed = max(1, used // 4)
        passed = fixed + (places - fixed + offset_by * (used - fixed)) % max(1, number_of - fixed)
        return jnp.zeros((number_of,), jnp.int32).at[order[jnp.where(places < fixed, places, passed)]].set(jnp.asarray(sizes, jnp.int32))

    sizes = jnp.where(number % 4 == 0, named(packed, number // 4), named(usual, number - number // 4 - 1))
    mixed = jax.random.permutation(jax.random.fold_in(own, 3), number_of)
    donor, sink = mixed[0:number_of // 2 * 2:2], mixed[1:number_of // 2 * 2:2]
    slack = jnp.minimum(sizes[donor] - 1, limit - sizes[sink]) // 2
    slack = jnp.where((donor == order[0]) | (sink == order[0]) | (sizes[sink] == 0), 0, jnp.maximum(slack, 0))
    passed = jax.random.randint(jax.random.fold_in(own, 4), (number_of // 2,), 0, 1 << 20) % (slack + 1)
    sizes = sizes.at[donor].add(-passed).at[sink].add(passed)
    labels = jnp.searchsorted(jnp.cumsum(sizes), jnp.arange(rows * top), side="right").astype(jnp.int32)
    table = labels.reshape(top, rows).T
    table = table[jax.random.permutation(jax.random.fold_in(own, 1), rows)]
    offset_by = jax.random.randint(jax.random.fold_in(own, 2), (rows, 1), 0, top)
    return jnp.take_along_axis(table, (jnp.arange(top)[None, :] + offset_by) % top, axis=1)


def portions_of(count, total, bound, lean, full):
    weights = [(1 << 20) // math.isqrt(rank ** lean) + 1 for rank in range(1, count + 1)]
    largest = bound if full else min(bound, max(-(-total // count), total * weights[0] // sum(weights)))
    least = 1 if total - largest >= count - 1 else 0
    given, surplus = [largest] + [least] * (count - 1), total - largest - least * (count - 1)
    while surplus > 0:
        candidates = [i for i in range(1, count) if given[i] < largest] or [i for i in range(1, count) if given[i] < bound]
        pool, remaining = sum([weights[i] for i in candidates]), surplus
        for i in candidates:
            more = min(bound - given[i], max(1, remaining * weights[i] // pool), surplus)
            given[i] = given[i] + more
            surplus = surplus - more
    return np.array(given)


def noise(own_key, dims, spread, most, shards=(), held_as=jnp.bfloat16):
    factor_of = block_levels(own_key, dims, shards, -0.22, 0.18) if shards else 1.0
    entries = jax.random.normal(own_key, dims, jnp.float32) * spread * factor_of
    return jnp.minimum(jnp.maximum(entries, -most), most).astype(held_as)


def setup_inputs(seed: int = 0) -> dict:
    key_of = jax.random.split(jax.random.key(seed), 9)
    disp = noise(key_of[0], (3, N_DEV * NODE_DEV), 1.0, 6.0, ((1, 128),), jnp.float32)
    probe = noise(key_of[1], (3, N_DEV * NODE_DEV), 1.0, 6.0, ((1, 128),), jnp.float32)
    strain_disp = noise(key_of[2], (6, 24, POINTS), 24 ** -0.5, 1.25, ((2, 128),), jnp.float32)
    conn = with_ends(jax.random.randint(key_of[3], (8, POINTS), 0, NODE_DEV + 2 * HALO), jax.random.fold_in(key_of[3], 1), 0, (NODE_DEV + 2 * HALO) - 1).astype(jnp.int32)
    halo_rows = with_ends(jax.random.randint(key_of[4], (N_DEV * 2 * HALO,), 0, NODE_DEV), jax.random.fold_in(key_of[4], 1), 0, NODE_DEV - 1).astype(jnp.int32)
    owner_keys = jax.random.split(jax.random.fold_in(key_of[5], 1), POINTS // POINTS)
    owner_turns = jax.random.permutation(jax.random.fold_in(key_of[5], 3), POINTS // POINTS)
    owner = jax.vmap(lambda own, number: shared_out(jax.random.fold_in(key_of[5], 2), own, number, POINTS, N_DEV, 1, OWN_MAX, 2))(owner_keys, owner_turns).reshape((POINTS, 1))
    counts = with_ends(jax.random.randint(key_of[6], (POINTS,), 1, ITER_HI + 1), jax.random.fold_in(key_of[6], 1), 1, ITER_HI).astype(jnp.int32)
    phase = with_ends((jax.random.randint(key_of[7], (N_DEV, VOX), 0, 3) < 1).astype(jnp.int32), jax.random.fold_in(key_of[7], 1), 0, 1)
    return dict(disp=disp, probe=probe, strain_disp=strain_disp, conn=conn, halo_rows=halo_rows, owner=owner, counts=counts, phase=phase)


PRECISE = lax.Precision.HIGHEST
ROOT_TWO = 1.4142135623730951
KAPPA_FERRITE = 2.0
SHEAR_FERRITE = 1.0
SOFT_FERRITE = 0.4
KAPPA_MARTENSITE = 2.4
SHEAR_MARTENSITE = 1.3
SOFT_MARTENSITE = 2.5
KAPPA_MEDIUM = 2.2
SHEAR_MEDIUM = 0.75
LAME_MEDIUM = KAPPA_MEDIUM - 2.0 * SHEAR_MEDIUM / 3.0
COUPLING = (LAME_MEDIUM + SHEAR_MEDIUM) / (LAME_MEDIUM + 2.0 * SHEAR_MEDIUM)

def directions(edge):
    index = jnp.arange(edge ** 3, dtype=jnp.int32)
    parts = [index // (edge * edge), index // edge % edge, index % edge]
    freqs = [jnp.where(k < edge // 2, k, k - edge).astype(jnp.float32) for k in parts]
    length = jnp.sqrt(jnp.maximum(freqs[0] ** 2 + freqs[1] ** 2 + freqs[2] ** 2, 1.0))
    return jnp.stack([f / length for f in freqs])

def polarize(tau, normal):
    first, second, third = (normal[0], normal[1], normal[2])
    trac_a = tau[0] * first + tau[5] / ROOT_TWO * second + tau[4] / ROOT_TWO * third
    trac_b = tau[5] / ROOT_TWO * first + tau[1] * second + tau[3] / ROOT_TWO * third
    trac_c = tau[4] / ROOT_TWO * first + tau[3] / ROOT_TWO * second + tau[2] * third
    along = first * trac_a + second * trac_b + third * trac_c
    vec_a = (trac_a - COUPLING * along * first) / SHEAR_MEDIUM
    vec_b = (trac_b - COUPLING * along * second) / SHEAR_MEDIUM
    vec_c = (trac_c - COUPLING * along * third) / SHEAR_MEDIUM
    return jnp.stack([first * vec_a, second * vec_b, third * vec_c, (second * vec_c + third * vec_b) / ROOT_TWO, (first * vec_c + third * vec_a) / ROOT_TWO, (first * vec_b + second * vec_a) / ROOT_TWO])

def material(strain, kappa, shear, soft):
    unit = jnp.array([1.0, 1.0, 1.0, 0.0, 0.0, 0.0], jnp.float32)[:, None]
    trace = strain[0] + strain[1] + strain[2]
    deviator = strain - unit * (trace / 3.0)
    squares = lax.optimization_barrier(jnp.sum(deviator * deviator, axis=0))
    factor = 1.0 / jnp.sqrt(1.0 + squares / (soft * soft))
    stress = unit * (kappa * trace) + 2.0 * shear * factor * deviator
    return (stress, deviator, factor)

def homogenize(field, kappa, shear, soft):
    stress, deviator, factor = material(field, kappa, shear, soft)
    unit = jnp.array([1.0, 1.0, 1.0, 0.0, 0.0, 0.0], jnp.float32)
    outer = unit[:, None] * unit[None, :]
    project = jnp.eye(6, dtype=jnp.float32) - outer / 3.0
    weight = 2.0 * shear * factor ** 3 / (soft * soft)
    tangent = jnp.mean(kappa) * outer + 2.0 * jnp.mean(shear * factor) * project
    tangent = tangent - jnp.dot(deviator * weight, deviator.T, precision=PRECISE) / field.shape[1]
    return (lax.optimization_barrier(jnp.mean(stress, axis=1)), tangent)

def phase_params(pattern):
    hard = pattern == 1
    kappa = jnp.where(hard, KAPPA_MARTENSITE, KAPPA_FERRITE).astype(jnp.float32)
    shear = jnp.where(hard, SHEAR_MARTENSITE, SHEAR_FERRITE).astype(jnp.float32)
    soft = jnp.where(hard, SOFT_MARTENSITE, SOFT_FERRITE).astype(jnp.float32)
    return (kappa, shear, soft)

def correction(field, kappa, shear, soft, normal):
    stress = material(field, kappa, shear, soft)[0]
    spectrum = jnp.fft.fftn(stress.reshape(6, NV, NV, NV), axes=(1, 2, 3)).reshape(6, VOX)
    real_part = polarize(jnp.real(spectrum), normal)
    imag_part = polarize(jnp.imag(spectrum), normal)
    back = jnp.fft.ifftn((real_part + 1j * imag_part).reshape(6, NV, NV, NV), axes=(1, 2, 3))
    return jnp.real(back).reshape(6, VOX)

def reference(disp, probe, strain_disp, conn, halo_rows, owner, counts, phase):
    ext_nodes = NODE_DEV + 2 * HALO
    fields = jnp.concatenate([disp, probe], axis=0).reshape(6, N_DEV, NODE_DEV)
    rows = halo_rows.reshape(N_DEV, 2 * HALO)
    send = jnp.take_along_axis(fields, rows[None], axis=2)
    zero = jnp.zeros((6, 1, HALO), jnp.float32)
    lower = jnp.concatenate([zero, send[:, :-1, HALO:]], axis=1)
    upper = jnp.concatenate([send[:, 1:, :HALO], zero], axis=1)
    extended = jnp.concatenate([fields, lower, upper], axis=2)
    links = conn.reshape(8, N_DEV, PT_DEV).transpose(1, 0, 2).reshape(N_DEV, 8 * PT_DEV)
    values = jnp.take_along_axis(extended, links[None], axis=2).reshape(6, N_DEV, 8, PT_DEV)
    values = values.transpose(0, 2, 1, 3).reshape(6, 8, POINTS)
    elem_u = values[:3].transpose(1, 0, 2).reshape(24, POINTS)
    elem_v = values[3:].transpose(1, 0, 2).reshape(24, POINTS)
    strain = jnp.einsum('ijp,jp->ip', strain_disp, elem_u, precision=PRECISE)
    dstrain = jnp.einsum('ijp,jp->ip', strain_disp, elem_v, precision=PRECISE)
    normal = directions(NV)

    def solve_point(item):
        mean_strain, count, owner_id = item
        pattern = lax.dynamic_index_in_dim(phase, owner_id, 0, keepdims=False)
        kappa, shear, soft = phase_params(pattern)
        field = jnp.broadcast_to(mean_strain[:, None], (6, VOX))
        for step in range(ITER_HI):
            update = field - correction(field, kappa, shear, soft, normal)
            field = jnp.where(step < count, update, field)
        return homogenize(field, kappa, shear, soft)
    stresses, tangents = lax.map(solve_point, (strain.T, counts, owner[:, 0]))
    point_stress = stresses.T
    images = jnp.einsum('pij,jp->ip', tangents, dstrain, precision=PRECISE)
    force_terms = jnp.einsum('ikp,ip->kp', strain_disp, point_stress, precision=PRECISE)
    image_terms = jnp.einsum('ikp,ip->kp', strain_disp, images, precision=PRECISE)
    force_terms = force_terms.reshape(8, 3, POINTS).transpose(1, 0, 2)
    image_terms = image_terms.reshape(8, 3, POINTS).transpose(1, 0, 2)
    terms = jnp.concatenate([force_terms, image_terms], axis=0).reshape(6, 8, N_DEV, PT_DEV)
    terms = terms.transpose(0, 2, 1, 3).reshape(6, N_DEV * 8 * PT_DEV)
    part_ids = jnp.arange(N_DEV, dtype=jnp.int32)[:, None]
    flat = (part_ids * ext_nodes + links).reshape(-1)
    acc = jnp.zeros((6, N_DEV * ext_nodes), jnp.float32).at[:, flat].add(terms)
    acc = acc.reshape(6, N_DEV, ext_nodes)
    back = acc[:, :, NODE_DEV:]
    from_lower = jnp.concatenate([zero, back[:, :-1, HALO:]], axis=1)
    from_upper = jnp.concatenate([back[:, 1:, :HALO], zero], axis=1)
    received = jnp.concatenate([from_lower, from_upper], axis=2).reshape(6, N_DEV * 2 * HALO)
    own_flat = (part_ids * NODE_DEV + rows).reshape(-1)
    own = acc[:, :, :NODE_DEV].reshape(6, N_DEV * NODE_DEV).at[:, own_flat].add(received)
    return (point_stress, own[:3], own[3:])
```

```python
import functools

import jax
import jax.numpy as jnp
import ml_dtypes
import numpy as np
from jax import lax
from jax.experimental import pallas as pl
from jax.experimental.pallas import tpu as pltpu
from jax.sharding import PartitionSpec as P

MERGED = False

EXACT = lax.Precision.HIGHEST
F32 = jnp.float32
BF16 = jnp.bfloat16
MESH = pl.DeviceIdType.MESH
VOXELS = 32768
ROOT_TWO = 1.4142135623730951
KAPPA = (2.0, 2.4)
SHEAR = (1.0, 1.3)
SOFT = (0.4, 2.5)
KAPPA_MEDIUM = 2.2
SHEAR_MEDIUM = 0.75
LAME_MEDIUM = KAPPA_MEDIUM - 2.0 * SHEAR_MEDIUM / 3.0
COUPLING = (LAME_MEDIUM + SHEAR_MEDIUM) / (LAME_MEDIUM + 2.0 * SHEAR_MEDIUM)
UPPER = [(i, j) for i in range(6) for j in range(i, 6)]
NONE = 4096.0


def two_parts(table):
    high = table.astype(np.float32).astype(ml_dtypes.bfloat16)
    low = (table - high.astype(np.float64)).astype(np.float32).astype(ml_dtypes.bfloat16)
    return high, low


def dft_tables():
    n32, n8, n4 = np.arange(32), np.arange(8), np.arange(4)
    f32 = np.exp(-2j * np.pi / 32 * np.outer(n32, n32))
    f8 = np.exp(-2j * np.pi / 8 * np.outer(n8, n8))
    f4 = np.exp(-2j * np.pi / 4 * np.outer(n4, n4))
    left = np.einsum("ab,cd->cabd", f32, f8).reshape(256, 256)
    left = np.block([[left.real, -left.imag], [left.imag, left.real]])
    rights = []
    for k0 in range(8):
        turn = np.exp(-2j * np.pi / 32 * n4 * k0)[:, None] * f4
        one = np.einsum("ab,cd->acbd", turn, f32).reshape(128, 128)
        rights.append(np.block([[one.real, one.imag], [-one.imag, one.real]]))
    right = np.stack(rights)
    return left, right, left.T / VOXELS, right.transpose(0, 2, 1)


def green_tables():
    row, lane = np.arange(256)[:, None], np.arange(128)[None, :]
    k = [row % 32 + 0 * lane, 8 * (lane // 32) + row // 32, lane % 32 + 0 * row]
    freq = [np.where(v < 16, v, v - 32).astype(np.float64) for v in k]
    length = np.sqrt(np.maximum(sum(f * f for f in freq), 1.0))
    normal = [f / length for f in freq]
    edge = [v == 16 for v in k]
    pairs = [(0, 0), (1, 1), (2, 2), (1, 2), (0, 2), (0, 1)]
    both = [
        normal[i] * normal[j] * (1.0 if i == j else ROOT_TWO) / SHEAR_MEDIUM for i, j in pairs
    ]
    even = [np.where(edge[i] == edge[j], v, 0.0) for (i, j), v in zip(pairs, both)]
    odd = [np.where(edge[i] == edge[j], 0.0, v) for (i, j), v in zip(pairs, both)][3:]
    return np.stack(even + odd).astype(np.float32)


def message_tables():
    spread = np.zeros((2, 2, 128, 128), np.float32)
    for uv in range(2):
        for d in range(3):
            for j in range(12):
                spread[uv, 0, 16 * d + 12 + uv, 32 + 16 * d + j] = 1.0
                spread[uv, 1, 16 * d + 14 + uv, 80 + 16 * d + j] = 1.0
    splat = np.zeros((128, 6, 128), np.float32)
    expand = np.zeros((128, 128), np.float32)
    for g in range(8):
        for i in range(6):
            for p in range(2):
                splat[16 * g + 2 * i + p, i, :] = 1.0
                for k in range(6):
                    expand[16 * g + 2 * i + p, 8 + 6 * i + k] = 1.0
    deal = np.zeros((2, 128, 128), np.float32)
    for i in range(6):
        for p in range(2):
            for lead in [0] + [32 + 16 * g for g in range(6)]:
                deal[0, i, lead + 2 * i + p] = 1.0
                for j in range(6):
                    deal[1, 8 + 6 * j + i, lead + 2 * i + p] = 1.0
    pack = lambda a: a.transpose(1, 0, 2).reshape(128, -1)
    return pack(spread[0]), splat.reshape(128, 768), pack(spread[1]), expand, pack(deal)


def summary_table():
    table = np.zeros((2, 32, 8, 128), np.float64)
    unit = np.array([1.0, 1, 1, 0, 0, 0])
    outer = np.outer(unit, unit)
    project = np.eye(6) - outer / 3.0
    for q in range(2):
        for i in range(6):
            table[q, 0, :, 64 * q + i] = unit[i]
            table[q, 1 + i, :, 64 * q + i] = 1.0
            for j in range(6):
                lane = 64 * q + 8 + 6 * j + i
                table[q, 29, :, lane] = outer[i, j]
                table[q, 7, :, lane] = 2.0 * project[i, j]
                place = UPPER.index((min(i, j), max(i, j)))
                table[q, 8 + place, :, lane] = -1.0
    return (table.reshape(512, 128) / VOXELS).astype(np.float32)


def iota(shape, dim):
    return lax.broadcasted_iota(jnp.int32, shape, dim)


def lanes_f32():
    return iota((8, 128), 1).astype(F32)


def exact_dot(a, b):
    return jnp.dot(a, b, precision=EXACT, preferred_element_type=F32)


def split(value):
    high = value.astype(BF16)
    return high, (value - high.astype(F32)).astype(BF16)


def dot3(a_high, a_low, b_high, b_low):
    out = jnp.dot(a_high, b_high, preferred_element_type=F32)
    out = out + jnp.dot(a_low, b_high, preferred_element_type=F32)
    return out + jnp.dot(a_high, b_low, preferred_element_type=F32)


def plane_peer(other):
    dev = lax.axis_index("dev")
    return (dev // 16) * 16 + (dev + other) % 16


def column_peer(other):
    return (lax.axis_index("dev") + 16 * other) % 128


def greet(both_cores):
    barrier = pltpu.get_barrier_semaphore()
    grp = lax.axis_index("grp")
    peers = [(grp, plane_peer(j)) for j in range(1, 16)]
    peers += [(grp, column_peer(j)) for j in range(1, 8)]
    if both_cores:
        peers += [((grp + 1) % 2, plane_peer(j)) for j in range(16)]
    for peer in peers:
        pl.semaphore_signal(barrier, inc=1, device_id=peer, device_id_type=MESH)
    pl.semaphore_wait(barrier, len(peers))


def copy_to(src, dst, send, recv, peer):
    return pltpu.make_async_remote_copy(
        src_ref=src, dst_ref=dst, send_sem=send, recv_sem=recv,
        device_id=peer, device_id_type=MESH,
    )


def gather_start(rows, row, cores, sems):
    dev, grp = lax.axis_index("dev"), lax.axis_index("grp")
    level = dev // 16
    mine = dev % 16 + (16 * grp if cores == 2 else 0)
    rows[level, pl.ds(mine, 1), :] = row
    copies = []
    for core in range(cores):
        for j in range(1 - core, 16):
            peer = ((grp + core) % 2, plane_peer(j))
            n = 16 * core + j
            here = rows.at[level, pl.ds(mine, 1)]
            copies.append(copy_to(here, here, sems[0].at[n], sems[1].at[n], peer))
    for copy in copies:
        copy.start()
    return copies


def gather_across(rows, sems):
    level, grp = lax.axis_index("dev") // 16, lax.axis_index("grp")
    here = rows.at[level]
    copies = [
        copy_to(here, here, sems[2].at[j], sems[3].at[j], (grp, column_peer(j)))
        for j in range(1, 8)
    ]
    for copy in copies:
        copy.start()
    return copies


def wait_all(copies):
    for copy in copies:
        copy.wait()


def widened(b_ref, conn_ref, d):
    del conn_ref
    parts = [b_ref[i, pl.ds(d, 8, stride=3), :] for i in range(6)]
    parts.append(jnp.zeros((8, 116), F32))
    return jnp.concatenate(parts, axis=1)


def partition_row(disp, probe, b_ref, conn_ref, listed, near_ref):
    lane, sub = iota((8, 128), 1), iota((8, 128), 0)
    conn = conn_ref[...]
    conn = jnp.concatenate([conn] * 6 + [jnp.full((8, 116), -1, jnp.int32)], axis=1)
    weights = [widened(b_ref, conn_ref, d) for d in range(3)]
    total = jnp.zeros((8, 128), F32)
    for uv, field in enumerate((disp, probe)):
        base = jnp.zeros((8, 128), F32)
        for d in range(3):
            value = jnp.zeros((8, 128), F32)
            for n in range(4):
                value = jnp.where(conn == n, field[d, n], value)
            base = base + weights[d] * value
        total = total + (pltpu.roll(base, 16, 1) if uv else base)
    for end in range(2):
        for d in range(3):
            one = jnp.where(conn == 4 + end, weights[d], 0.0)
            total = total + pltpu.roll(one, 32 + 48 * end + 16 * d, 1)
    row = jnp.sum(total, axis=0, keepdims=True)
    for d in range(3):
        for uv, field in enumerate((disp, probe)):
            for way in range(2):
                value = jnp.zeros((1, 128), F32)
                for n in range(4):
                    value = jnp.where(
                        jnp.full((1, 128), listed[1 - way], jnp.int32) == n, field[d, n], value
                    )
                row = jnp.where(lane[:1] == 16 * d + 12 + 2 * way + uv, value, row)
    for n in range(4):
        near = jnp.zeros((8, 128), F32)
        for d in range(3):
            one = jnp.sum(jnp.where(conn == n, weights[d], 0.0), axis=0, keepdims=True)
            near = jnp.where(sub == d, one, near)
        near_ref[n] = near
    return row


def point_rows(rows, point, uv, spread):
    lane = lanes_f32()
    part = jnp.floor(point * 0.5)
    parity = point - 2.0 * part
    pick = jnp.concatenate([lane == part, lane == part - 1.0, lane == part + 1.0], axis=0)
    found = exact_dot(pick.astype(F32), rows)
    below = exact_dot(found[8:16], spread[:, :128])
    above = exact_dot(found[16:24], spread[:, 128:])
    count = iota((8, 128), 1)
    base = ((count // 16) == uv).astype(F32)
    own = (count % 2).astype(F32) == parity
    factor = jnp.where((count % 16) < 12, base + below + above, 0.0)
    return found[:8], jnp.where(own, found[:8] * factor, 0.0)


def my_points(owner, counts):
    me, grp = lax.axis_index("dev"), lax.axis_index("grp")
    index = iota((1, 256), 1).astype(F32)
    mine = owner == me
    first = jnp.min(jnp.where(mine, index, NONE), axis=1, keepdims=True)
    second = jnp.min(jnp.where(mine & (index > first), index, NONE), axis=1, keepdims=True)
    third = jnp.min(jnp.where(mine & (index > second), index, NONE), axis=1, keepdims=True)
    even = jnp.full((1, 1), grp, jnp.int32) == 0
    slots = (jnp.where(even, first, second), jnp.where(even, third, NONE))
    sub = iota((8, 128), 0)
    point = jnp.where(sub == 0, slots[0], jnp.where(sub == 1, slots[1], NONE))
    turns = [
        jnp.sum(jnp.where(index == slot, counts.astype(F32), 0.0), axis=1, keepdims=True)
        for slot in slots
    ]
    return point, turns


def green(tau, t, odd):
    half = [0.5 * t[q] for q in (3, 4, 5)]
    cross = [v * (1.0 / ROOT_TWO) for v in half]
    p3, p4, p5 = (half[0] * tau[3], half[1] * tau[4], half[2] * tau[5])
    d0, d1, d2 = (t[0] * tau[0], t[1] * tau[1], t[2] * tau[2])
    along = (COUPLING * SHEAR_MEDIUM) * (d0 + d1 + d2 + 2.0 * (p3 + p4 + p5))
    aside = (COUPLING * SHEAR_MEDIUM) * (odd[0] * tau[3] + odd[1] * tau[4] + odd[2] * tau[5])
    s12, s02, s01 = (0.5 * (t[1] + t[2]), 0.5 * (t[0] + t[2]), 0.5 * (t[0] + t[1]))
    return [
        d0 + p5 + p4 - along * t[0],
        d1 + p5 + p3 - along * t[1],
        d2 + p4 + p3 - along * t[2],
        cross[2] * tau[4] + cross[1] * tau[5] + half[0] * (tau[1] + tau[2]) + s12 * tau[3]
        - along * t[3] - aside * odd[0],
        cross[2] * tau[3] + cross[0] * tau[5] + half[1] * (tau[0] + tau[2]) + s02 * tau[4]
        - along * t[4] - aside * odd[1],
        cross[1] * tau[3] + cross[0] * tau[4] + half[2] * (tau[0] + tau[1]) + s01 * tau[5]
        - along * t[5] - aside * odd[2],
    ]


def law(e, kappa, shear, scale):
    trace = e[0] + e[1] + e[2]
    third = trace * (1.0 / 3.0)
    dev = [e[i] - third for i in range(3)] + list(e[3:])
    size = dev[0] * dev[0]
    for v in dev[1:]:
        size = size + v * v
    factor = lax.rsqrt(1.0 + size * scale)
    return kappa * trace, dev, 2.0 * shear * factor, factor


def by_phase(hard, pair):
    return jnp.where(hard, pair[1], pair[0])


def materials(hard):
    return (
        by_phase(hard, KAPPA), by_phase(hard, SHEAR),
        by_phase(hard, (1.0 / SOFT[0] ** 2, 1.0 / SOFT[1] ** 2)),
    )


def phase_spectrum(c):
    pattern = (c.phase[...] == 1).astype(F32).astype(BF16)
    z = jnp.dot(c.lf_h[:, :256], pattern, preferred_element_type=F32)
    z = z + jnp.dot(c.lf_l[:, :256], pattern, preferred_element_type=F32)
    for k in range(8):
        rows = jnp.concatenate([z[32 * k : 32 * k + 32], z[256 + 32 * k : 288 + 32 * k]], axis=1)
        high, low = split(rows)
        c.chi[pl.ds(32 * k, 32), :] = dot3(high, low, c.rf_h[k], c.rf_l[k])


def back_right(c, k):
    high, low = split(c.spec[...])
    w = dot3(high, low, c.ri_h[k], c.ri_l[k])
    high, low = split(w)
    for q in range(6):
        for part in range(2):
            at = (pl.ds(pl.multiple_of(256 * part + 32 * k, 32), 32), pl.ds(128 * q, 128))
            from_ = (slice(32 * q, 32 * q + 32), slice(128 * part, 128 * part + 128))
            c.x_h[at] = high[from_]
            c.x_l[at] = low[from_]


def left(c, high, low, out):
    for q in range(3):
        cols = pl.ds(256 * q, 256)
        out[:, cols] = dot3(high[...], low[...], c.x_h[:, cols], c.x_l[:, cols])


def solve(c, e, turns):
    jumps = []
    for q in range(2):
        ends = []
        for m in range(2):
            kt, dev, stiff, _ = law(e[q], KAPPA[m], SHEAR[m], 1.0 / SOFT[m] ** 2)
            ends.append([stiff * v + (kt if i < 3 else 0.0) for i, v in enumerate(dev)])
        jumps.append([b - a for a, b in zip(*ends)])

    def first(k, carry):
        for part in range(4):
            at = pl.multiple_of(32 * k + 8 * part, 8)
            t = [c.green[q, pl.ds(at, 8), :] for q in range(9)]
            real, imag = c.chi[pl.ds(at, 8), :128], c.chi[pl.ds(at, 8), 128:]
            one, two = green(jumps[0], t[:6], t[6:]), green(jumps[1], t[:6], t[6:])
            for q in range(6):
                rows = slice(32 * q + 8 * part, 32 * q + 8 * part + 8)
                c.spec[rows, :128] = real * one[q] - imag * two[q]
                c.spec[rows, 128:] = real * two[q] + imag * one[q]
        back_right(c, k)
        return carry

    lax.fori_loop(0, 8, first, 0)
    left(c, c.li_h, c.li_l, c.u)

    def stress(r, carry):
        at = pl.multiple_of(16 * r, 16)
        kappa, shear, scale = materials(c.phase[pl.ds(at, 16), :] == 1)
        for q in range(2):
            rows = pl.ds(pl.multiple_of(256 * q + 16 * r, 16), 16)
            field = [
                jnp.concatenate([e[q][i]] * 2, axis=0) - c.u[rows, pl.ds(128 * i, 128)]
                for i in range(6)
            ]
            kt, dev, stiff, _ = law(field, kappa, shear, scale)
            for i in range(6):
                c.f[rows, pl.ds(128 * i, 128)] = field[i]
                high, low = split(stiff * dev[i] + (kt if i < 3 else 0.0))
                c.x_h[rows, pl.ds(128 * i, 128)] = high
                c.x_l[rows, pl.ds(128 * i, 128)] = low
        return carry

    lax.fori_loop(0, 16, stress, 0)
    left(c, c.lf_h, c.lf_l, c.u)

    def middle(k, carry):
        near, far = pl.multiple_of(32 * k, 32), pl.multiple_of(256 + 32 * k, 32)
        rows = jnp.concatenate(
            [
                jnp.concatenate(
                    [c.u[pl.ds(near, 32), pl.ds(128 * q, 128)], c.u[pl.ds(far, 32), pl.ds(128 * q, 128)]],
                    axis=1,
                )
                for q in range(6)
            ],
            axis=0,
        )
        high, low = split(rows)
        c.spec[...] = dot3(high, low, c.rf_h[k], c.rf_l[k])
        for part in range(4):
            at = pl.multiple_of(32 * k + 8 * part, 8)
            t = [c.green[q, pl.ds(at, 8), :] for q in range(9)]
            for half in range(2):
                cols = slice(128 * half, 128 * half + 128)
                spots = [slice(32 * q + 8 * part, 32 * q + 8 * part + 8) for q in range(6)]
                out = green([c.spec[s, cols] for s in spots], t[:6], t[6:])
                for s, v in zip(spots, out):
                    c.spec[s, cols] = v
        back_right(c, k)
        return carry

    lax.fori_loop(0, 8, middle, 0)
    left(c, c.li_h, c.li_l, c.u)

    for q in range(2):
        keep = jnp.broadcast_to((turns[q] > 1.5).astype(F32), (8, 128))

        def total(r, sums, q=q, keep=keep):
            at = pl.multiple_of(8 * r, 8)
            kappa, shear, scale = materials(c.phase[pl.ds(at, 8), :] == 1)
            rows = pl.ds(pl.multiple_of(256 * q + 8 * r, 8), 8)
            field = [
                c.f[rows, pl.ds(128 * i, 128)] - keep * c.u[rows, pl.ds(128 * i, 128)]
                for i in range(6)
            ]
            kt, dev, stiff, factor = law(field, kappa, shear, scale)
            weight = stiff * factor * factor * scale
            heavy = [weight * v for v in dev]
            new = [kt] + [stiff * v for v in dev] + [shear * factor]
            new += [heavy[i] * dev[j] for i, j in UPPER] + [kappa]
            return tuple(s + v for s, v in zip(sums, new))

        sums = lax.fori_loop(0, 32, total, (jnp.zeros((8, 128), F32),) * 30)
        for n, v in enumerate(sums):
            c.sums[pl.ds(256 * q + 8 * n, 8), :] = v
        c.sums[pl.ds(256 * q + 240, 16), :] = jnp.zeros((16, 128), F32)
    ones = jnp.ones((8, 128), F32)
    lanes = lax.dot_general(
        ones, c.sums[...], (((1,), (1,)), ((), ())), precision=EXACT, preferred_element_type=F32
    )
    return exact_dot(lanes, c.summary[...])


def finish(rows, results, owner, listed, near, c, stress_ref, force_ref, image_ref):
    dev = lax.axis_index("dev")
    sub, lane = iota((8, 128), 0), iota((8, 128), 1)
    step = jnp.where(sub < 2, 0, jnp.where(sub < 4, -1, 1))
    point = (2 * (jnp.full((8, 128), dev, jnp.int32) + step) + sub % 2).astype(F32)
    point = jnp.where(sub < 6, point, NONE)
    found, masked = point_rows(rows, point, 1, c.spread_v[...])
    direction = exact_dot(masked, c.expand[...])
    index = iota((8, 256), 1).astype(F32)
    wide = jnp.concatenate([point, point], axis=1)
    owners = jnp.broadcast_to(owner.astype(F32), (8, 256))
    who = jnp.sum(jnp.where(index == wide, owners, 0.0), axis=1, keepdims=True)
    rank = jnp.sum(
        jnp.where((owners == who) & (index < wide), 1.0, 0.0), axis=1, keepdims=True
    )
    slot = jnp.floor(rank * 0.5)
    level = jnp.floor(who * 0.0625)
    place = who + 16.0 * level + 16.0 * (rank - 2.0 * slot)
    value = exact_dot((index == place).astype(F32), results)
    value = jnp.where(slot > 0.5, pltpu.roll(value, 64, 1), value)
    value = jnp.where(lane < 64, value, 0.0)
    terms = value * jnp.where(lane < 6, 1.0, direction)
    dealt = exact_dot(terms, c.deal[...])
    own_lane = lane % 2 == sub % 2
    out_sub, out_lane = sub, lane
    column = jnp.where(out_lane == 0, value[0:1], 0.0)
    del column
    picks = [
        jnp.sum(jnp.where(out_lane == out_sub, value[p : p + 1], 0.0), axis=1, keepdims=True)
        for p in range(2)
    ]
    stress_ref[...] = jnp.where(out_lane == 0, picks[0], picks[1])[:6, :2]
    for half, ref in enumerate((force_ref, image_ref)):
        y = jnp.where(own_lane, dealt[:, 128 * half : 128 * half + 128], 0.0)
        mine = jnp.sum(jnp.where(sub < 2, y, 0.0), axis=0, keepdims=True)
        linked = y * found
        before = jnp.sum(jnp.where((sub == 2) | (sub == 3), linked, 0.0), axis=0, keepdims=True)
        after = jnp.sum(jnp.where((sub == 4) | (sub == 5), linked, 0.0), axis=0, keepdims=True)
        twelve = lane % 16 < 12
        out = jnp.zeros((8, 128), F32)
        for n in range(4):
            got = jnp.sum(near[n] * mine, axis=1, keepdims=True)
            out = jnp.where(lane == n, got, out)
        for end, row, lead in ((0, before, 5), (1, after, 2)):
            part = jnp.where(twelve & (lane // 16 == sub + lead) & (sub < 3), row, 0.0)
            got = jnp.sum(part, axis=1, keepdims=True)
            out = out + jnp.where(lane == listed[end], got, 0.0)
        ref[...] = out[:3, :4]


TABLES = ("lf_h", "lf_l", "li_h", "li_l", "rf_h", "rf_l", "ri_h", "ri_l", "green")
SMALL = ("spread_u", "splat", "summary", "spread_v", "expand", "deal")
WORK = {
    "chi": ((256, 256), F32),
    "spec": ((192, 256), F32),
    "x_h": ((512, 768), BF16),
    "x_l": ((512, 768), BF16),
    "u": ((512, 768), F32),
    "f": ((512, 768), F32),
    "sums": ((512, 128), F32),
}


class Bag:
    def __init__(self, **refs):
        self.__dict__.update(refs)


def constants():
    lf, rf, li, ri = dft_tables()
    out = {"green": green_tables(), "summary": summary_table()}
    for name, table in (("lf", lf), ("li", li), ("rf", rf), ("ri", ri)):
        out[name + "_h"], out[name + "_l"] = two_parts(table)
    names = ("spread_u", "splat", "spread_v", "expand", "deal")
    out.update(zip(names, message_tables()))
    return out


def splats(rows, owner, counts, c):
    point, turns = my_points(owner, counts)
    _, masked = point_rows(rows, point, 0, c.spread_u[...])
    strain = exact_dot(masked, c.splat[...])
    e = [
        [jnp.broadcast_to(strain[q : q + 1, 128 * i : 128 * i + 128], (8, 128)) for i in range(6)]
        for q in range(2)
    ]
    return e, turns


VM = pl.BlockSpec(memory_space=pltpu.VMEM)
SM = pl.BlockSpec(memory_space=pltpu.SMEM)
SEMS = [
    pltpu.SemaphoreType.DMA((32,)), pltpu.SemaphoreType.DMA((32,)),
    pltpu.SemaphoreType.DMA((8,)), pltpu.SemaphoreType.DMA((8,)),
]


def first_kernel(disp, probe, b, conn, listed, rows_out, near_out, rows, *sems):
    row = partition_row(disp, probe, b, conn, listed, near_out)
    greet(False)
    wait_all(gather_start(rows, row, 1, sems))
    wait_all(gather_across(rows, sems))
    rows_out[...] = rows[...]


def second_kernel(names, *refs):
    c = Bag(**dict(zip(names, refs)))
    phase_spectrum(c)
    e, turns = splats(c.rows[...], c.owner[...], c.counts[...], c)
    c.out[...] = solve(c, e, turns)


def third_kernel(result, gathered, owner, listed, near, sv, ex, de, s_out, f_out, i_out, rows, *sems):
    c = Bag(spread_v=sv, expand=ex, deal=de)
    greet(True)
    wait_all(gather_start(rows, result[0:1, :], 2, sems))
    wait_all(gather_across(rows, sems))
    results = rows[...].reshape(256, 128)
    finish(gathered[...], results, owner[...], listed, near, c, s_out, f_out, i_out)


def on_device(disp, probe, strain_disp, conn, halo_rows, owner, counts, phase):
    table = {k: jnp.asarray(v) for k, v in constants().items()}
    owner, counts = owner.reshape(1, 256), counts.reshape(1, 256)
    phase = phase.reshape(256, 128)
    shape = jax.ShapeDtypeStruct
    rows, near = pl.pallas_call(
        first_kernel,
        out_shape=(shape((8, 16, 128), F32), shape((4, 8, 128), F32)),
        in_specs=[SM, SM, VM, VM, SM],
        out_specs=(VM, VM),
        scratch_shapes=[pltpu.VMEM((8, 16, 128), F32)] + SEMS,
        compiler_params=pltpu.CompilerParams(collective_id=0, has_side_effects=True),
    )(disp, probe, strain_disp, conn, halo_rows)
    rows = rows.reshape(128, 128)
    names = ("rows", "owner", "counts", "phase") + TABLES + SMALL[:3]
    args = [rows, owner, counts, phase] + [table[n] for n in TABLES + SMALL[:3]]
    result = pl.pallas_call(
        functools.partial(second_kernel, names + ("out",) + tuple(WORK)),
        out_shape=shape((8, 128), F32),
        in_specs=[VM] * len(args),
        out_specs=VM,
        scratch_shapes=[pltpu.VMEM(*v) for v in WORK.values()],
        compiler_params=pltpu.CompilerParams(vmem_limit_bytes=48 << 20),
    )(*args)
    outs = pl.pallas_call(
        third_kernel,
        out_shape=(shape((6, 2), F32), shape((3, 4), F32), shape((3, 4), F32)),
        in_specs=[VM, VM, VM, SM, VM, VM, VM, VM],
        out_specs=(VM, VM, VM),
        scratch_shapes=[pltpu.VMEM((8, 32, 128), F32)] + SEMS,
        compiler_params=pltpu.CompilerParams(collective_id=1, has_side_effects=True),
    )(result, rows, owner, halo_rows, near, *[table[n] for n in SMALL[3:]])
    return outs


def solution(mesh):
    dev = P(None, "dev")
    return jax.shard_map(
        on_device,
        mesh=mesh,
        in_specs=(dev, dev, P(None, None, "dev"), dev, P("dev"), P(), P(), P("dev", None)),
        out_specs=(dev, dev, dev),
        check_vma=False,
    )
```

```python
import jax
import jax.numpy as jnp
import ml_dtypes
import numpy as np
from jax import lax
from jax.experimental import pallas as pl
from jax.experimental.pallas import tpu as pltpu
from jax.sharding import PartitionSpec as P

EXACT = lax.Precision.HIGHEST
F32 = jnp.float32
BF16 = jnp.bfloat16
MESH = pl.DeviceIdType.MESH
VOXELS = 32768
ROOT_TWO = 1.4142135623730951
KAPPA = (2.0, 2.4)
SHEAR = (1.0, 1.3)
SOFT = (0.4, 2.5)
KAPPA_MEDIUM = 2.2
SHEAR_MEDIUM = 0.75
LAME_MEDIUM = KAPPA_MEDIUM - 2.0 * SHEAR_MEDIUM / 3.0
COUPLING = (LAME_MEDIUM + SHEAR_MEDIUM) / (LAME_MEDIUM + 2.0 * SHEAR_MEDIUM)
UPPER = [(i, j) for i in range(6) for j in range(i, 6)]
NONE = 4096.0


def two_parts(table):
    high = table.astype(np.float32).astype(ml_dtypes.bfloat16)
    low = (table - high.astype(np.float64)).astype(np.float32).astype(ml_dtypes.bfloat16)
    return high, low


def dft_tables():
    n32, n8, n4 = np.arange(32), np.arange(8), np.arange(4)
    f32 = np.exp(-2j * np.pi / 32 * np.outer(n32, n32))
    f8 = np.exp(-2j * np.pi / 8 * np.outer(n8, n8))
    f4 = np.exp(-2j * np.pi / 4 * np.outer(n4, n4))
    left = np.einsum("ab,cd->cabd", f32, f8).reshape(256, 256)
    left = np.block([[left.real, -left.imag], [left.imag, left.real]])
    rights = []
    for k0 in range(8):
        turn = np.exp(-2j * np.pi / 32 * n4 * k0)[:, None] * f4
        one = np.einsum("ab,cd->acbd", turn, f32).reshape(128, 128)
        rights.append(np.block([[one.real, one.imag], [-one.imag, one.real]]))
    right = np.stack(rights)
    return left, right, left.T / VOXELS, right.transpose(0, 2, 1)


def green_tables():
    row, lane = np.arange(256)[:, None], np.arange(128)[None, :]
    k = [row % 32 + 0 * lane, 8 * (lane // 32) + row // 32, lane % 32 + 0 * row]
    freq = [np.where(v < 16, v, v - 32).astype(np.float64) for v in k]
    length = np.sqrt(np.maximum(sum(f * f for f in freq), 1.0))
    normal = [f / length for f in freq]
    edge = [v == 16 for v in k]
    pairs = [(0, 0), (1, 1), (2, 2), (1, 2), (0, 2), (0, 1)]
    both = [
        normal[i] * normal[j] * (1.0 if i == j else ROOT_TWO) / SHEAR_MEDIUM for i, j in pairs
    ]
    even = [np.where(edge[i] == edge[j], v, 0.0) for (i, j), v in zip(pairs, both)]
    odd = [np.where(edge[i] == edge[j], 0.0, v) for (i, j), v in zip(pairs, both)][3:]
    return np.stack(even + odd).astype(np.float32)


def message_tables():
    spread = np.zeros((2, 2, 128, 128), np.float32)
    for uv in range(2):
        for d in range(3):
            for j in range(12):
                spread[uv, 0, 16 * d + 12 + uv, 32 + 16 * d + j] = 1.0
                spread[uv, 1, 16 * d + 14 + uv, 80 + 16 * d + j] = 1.0
    splat = np.zeros((128, 6, 128), np.float32)
    expand = np.zeros((128, 128), np.float32)
    for g in range(8):
        for i in range(6):
            for p in range(2):
                splat[16 * g + 2 * i + p, i, :] = 1.0
                for k in range(6):
                    expand[16 * g + 2 * i + p, 8 + 6 * i + k] = 1.0
    deal = np.zeros((2, 128, 128), np.float32)
    for i in range(6):
        for p in range(2):
            for lead in [0] + [32 + 16 * g for g in range(6)]:
                deal[0, i, lead + 2 * i + p] = 1.0
                for j in range(6):
                    deal[1, 8 + 6 * j + i, lead + 2 * i + p] = 1.0
    pack = lambda a: a.transpose(1, 0, 2).reshape(128, -1)
    return pack(spread[0]), splat.reshape(128, 768), pack(spread[1]), expand, pack(deal)


def summary_table():
    table = np.zeros((2, 32, 8, 128), np.float64)
    unit = np.array([1.0, 1, 1, 0, 0, 0])
    outer = np.outer(unit, unit)
    project = np.eye(6) - outer / 3.0
    for q in range(2):
        for i in range(6):
            table[q, 0, :, 64 * q + i] = unit[i]
            table[q, 1 + i, :, 64 * q + i] = 1.0
            for j in range(6):
                lane = 64 * q + 8 + 6 * j + i
                table[q, 29, :, lane] = outer[i, j]
                table[q, 7, :, lane] = 2.0 * project[i, j]
                place = UPPER.index((min(i, j), max(i, j)))
                table[q, 8 + place, :, lane] = -1.0
    return (table.reshape(512, 128) / VOXELS).astype(np.float32)


def iota(shape, dim):
    return lax.broadcasted_iota(jnp.int32, shape, dim)


def lanes_f32():
    return iota((8, 128), 1).astype(F32)


def exact_dot(a, b):
    return jnp.dot(a, b, precision=EXACT, preferred_element_type=F32)


def split(value):
    high = value.astype(BF16)
    return high, (value - high.astype(F32)).astype(BF16)


def dot3(a_high, a_low, b_high, b_low):
    out = jnp.dot(a_high, b_high, preferred_element_type=F32)
    out = out + jnp.dot(a_low, b_high, preferred_element_type=F32)
    return out + jnp.dot(a_high, b_low, preferred_element_type=F32)


FAR = (4, 5, 3, 6, 2, 7, 1, 0)


def each_peer(action):
    dev = lax.axis_index("dev")
    for across in FAR:
        level = (dev // 16 + across) % 8

        def one(j, carry, level=level):
            action(level * 16 + (dev + j) % 16)
            return carry

        lax.fori_loop(1 if across == 0 else 0, 16, one, 0)


def sibling():
    return ((lax.axis_index("grp") + 1) % 2, lax.axis_index("dev"))


def greet():
    barrier = pltpu.get_barrier_semaphore()
    grp = lax.axis_index("grp")

    def signal(peer):
        pl.semaphore_signal(barrier, inc=1, device_id=peer, device_id_type=MESH)

    each_peer(lambda dev: signal((grp, dev)))
    signal(sibling())
    return barrier


def gather_start(note, rows, send, recv):
    dev, grp = lax.axis_index("dev"), lax.axis_index("grp")
    src, dst = note.at[pl.ds(0, 1)], rows.at[pl.ds(dev, 1)]

    def start(peer):
        pltpu.make_async_remote_copy(
            src_ref=src, dst_ref=dst, send_sem=send, recv_sem=recv,
            device_id=(grp, peer), device_id_type=MESH,
        ).start()

    each_peer(start)
    pltpu.make_async_copy(src, dst, recv).start()


def gather_wait(rows, send, recv):
    pltpu.make_async_copy(rows, rows, recv).wait()
    most = rows.at[pl.ds(0, 127)]
    pltpu.make_async_copy(most, most, send).wait()


def partition_row(disp, probe, b_ref, conn_ref, listed, flat, near_ref):
    lane, sub = iota((8, 128), 1), iota((8, 128), 0)
    flat[...] = jnp.zeros((128, 128), F32)
    for i in range(6):
        flat[pl.ds(2 * i, 2), pl.ds(0, 24)] = b_ref[i]
    axis = lane % 3
    spread = (lane // 3 == sub).astype(F32)
    conn = jnp.dot(conn_ref[...].astype(F32), spread, preferred_element_type=F32)
    values = []
    for field in (disp, probe):
        values.append(
            [
                jnp.where(axis == 0, field[0, n], jnp.where(axis == 1, field[1, n], field[2, n]))
                for n in range(4)
            ]
        )
    blocks, nears = [], []
    for p in range(2):
        c = jnp.broadcast_to(conn[p : p + 1], (8, 128))
        block = ((c == 4.0) & (axis == sub - 2)) | ((c == 5.0) & (axis == sub - 5))
        block = block.astype(F32)
        for uv in range(2):
            value = jnp.zeros((8, 128), F32)
            for n in range(4):
                value = jnp.where(c == float(n), values[uv][n], value)
            block = jnp.where(sub == uv, value, block)
        blocks.append(block)
        nears.append([((c == float(n)) & (axis == sub)).astype(F32) for n in range(4)])
    heap = blocks + [nears[p][n] for n in range(4) for p in range(2)]
    w = lax.dot_general(
        jnp.concatenate(heap, axis=0), flat[...], (((1,), (1,)), ((), ())),
        precision=EXACT, preferred_element_type=F32,
    )
    even = lane % 2 == 0
    x = jnp.where(even, w[:8], w[8:16])
    total = jnp.where(sub == 0, x, 0.0)
    for g in range(1, 8):
        total = total + pltpu.roll(jnp.where(sub == g, x, 0.0), 16 * g, 1)
    row = jnp.sum(total, axis=0, keepdims=True)
    for n in range(4):
        at = 16 + 16 * n
        near_ref[n] = jnp.where(even, w[at : at + 8], w[at + 8 : at + 16])
    for way in range(2):
        want = jnp.full((1, 128), listed[1 - way], jnp.int32)
        for uv in range(2):
            sent = jnp.zeros((1, 128), F32)
            for n in range(4):
                field = (disp, probe)[uv]
                third = lane[:1] // 16
                value = jnp.where(
                    third == 0, field[0, n], jnp.where(third == 1, field[1, n], field[2, n])
                )
                sent = jnp.where(want == n, value, sent)
            place = (lane[:1] < 48) & (lane[:1] % 16 == 12 + 2 * way + uv)
            row = jnp.where(place, sent, row)
    return row


def point_rows(rows, point, uv, spread):
    lane = lanes_f32()
    part = jnp.floor(point * 0.5)
    parity = point - 2.0 * part
    pick = jnp.concatenate([lane == part, lane == part - 1.0, lane == part + 1.0], axis=0)
    found = exact_dot(pick.astype(F32), rows)
    below = exact_dot(found[8:16], spread[:, :128])
    above = exact_dot(found[16:24], spread[:, 128:])
    count = iota((8, 128), 1)
    base = ((count // 16) == uv).astype(F32)
    own = (count % 2).astype(F32) == parity
    factor = jnp.where((count % 16) < 12, base + below + above, 0.0)
    return found[:8], jnp.where(own, found[:8] * factor, 0.0)


def my_points(owner, counts):
    me, grp = lax.axis_index("dev"), lax.axis_index("grp")
    index = iota((1, 256), 1).astype(F32)
    mine = owner == me
    first = jnp.min(jnp.where(mine, index, NONE), axis=1, keepdims=True)
    second = jnp.min(jnp.where(mine & (index > first), index, NONE), axis=1, keepdims=True)
    third = jnp.min(jnp.where(mine & (index > second), index, NONE), axis=1, keepdims=True)
    even = jnp.full((1, 1), grp, jnp.int32) == 0
    slots = (jnp.where(even, first, second), jnp.where(even, third, NONE))
    sub = iota((8, 128), 0)
    point = jnp.where(sub == 0, slots[0], jnp.where(sub == 1, slots[1], NONE))
    turns = [
        jnp.sum(jnp.where(index == slot, counts.astype(F32), 0.0), axis=1, keepdims=True)
        for slot in slots
    ]
    return point, turns


def green(tau, t, odd):
    half = [0.5 * t[q] for q in (3, 4, 5)]
    cross = [v * (1.0 / ROOT_TWO) for v in half]
    p3, p4, p5 = (half[0] * tau[3], half[1] * tau[4], half[2] * tau[5])
    d0, d1, d2 = (t[0] * tau[0], t[1] * tau[1], t[2] * tau[2])
    along = (COUPLING * SHEAR_MEDIUM) * (d0 + d1 + d2 + 2.0 * (p3 + p4 + p5))
    aside = (COUPLING * SHEAR_MEDIUM) * (odd[0] * tau[3] + odd[1] * tau[4] + odd[2] * tau[5])
    s12, s02, s01 = (0.5 * (t[1] + t[2]), 0.5 * (t[0] + t[2]), 0.5 * (t[0] + t[1]))
    return [
        d0 + p5 + p4 - along * t[0],
        d1 + p5 + p3 - along * t[1],
        d2 + p4 + p3 - along * t[2],
        cross[2] * tau[4] + cross[1] * tau[5] + half[0] * (tau[1] + tau[2]) + s12 * tau[3]
        - along * t[3] - aside * odd[0],
        cross[2] * tau[3] + cross[0] * tau[5] + half[1] * (tau[0] + tau[2]) + s02 * tau[4]
        - along * t[4] - aside * odd[1],
        cross[1] * tau[3] + cross[0] * tau[4] + half[2] * (tau[0] + tau[1]) + s01 * tau[5]
        - along * t[5] - aside * odd[2],
    ]


def law(e, kappa, shear, scale):
    trace = e[0] + e[1] + e[2]
    third = trace * (1.0 / 3.0)
    dev = [e[i] - third for i in range(3)] + list(e[3:])
    size = dev[0] * dev[0]
    for v in dev[1:]:
        size = size + v * v
    factor = lax.rsqrt(1.0 + size * scale)
    return kappa * trace, dev, 2.0 * shear * factor, factor


def by_phase(hard, pair):
    return jnp.where(hard, pair[1], pair[0])


def materials(hard):
    return (
        by_phase(hard, KAPPA), by_phase(hard, SHEAR),
        by_phase(hard, (1.0 / SOFT[0] ** 2, 1.0 / SOFT[1] ** 2)),
    )


def phase_spectrum(c):
    pattern = (c.phase[...] == 1).astype(F32).astype(BF16)
    z = jnp.dot(c.lf_h[:, :256], pattern, preferred_element_type=F32)
    z = z + jnp.dot(c.lf_l[:, :256], pattern, preferred_element_type=F32)
    for k in range(8):
        rows = jnp.concatenate([z[32 * k : 32 * k + 32], z[256 + 32 * k : 288 + 32 * k]], axis=1)
        high, low = split(rows)
        c.chi[pl.ds(32 * k, 32), :] = dot3(high, low, c.rf_h[k], c.rf_l[k])


def back_right(c, k):
    high, low = split(c.spec[...])
    w = dot3(high, low, c.ri_h[k], c.ri_l[k])
    high, low = split(w)
    for q in range(6):
        for part in range(2):
            at = (pl.ds(pl.multiple_of(256 * part + 32 * k, 32), 32), pl.ds(128 * q, 128))
            from_ = (slice(32 * q, 32 * q + 32), slice(128 * part, 128 * part + 128))
            c.x_h[at] = high[from_]
            c.x_l[at] = low[from_]


def left(c, high, low, out):
    for q in range(3):
        cols = pl.ds(256 * q, 256)
        out[:, cols] = dot3(high[...], low[...], c.x_h[:, cols], c.x_l[:, cols])


def solve(c, e, turns):
    jumps = []
    for q in range(2):
        ends = []
        for m in range(2):
            kt, dev, stiff, _ = law(e[q], KAPPA[m], SHEAR[m], 1.0 / SOFT[m] ** 2)
            ends.append([stiff * v + (kt if i < 3 else 0.0) for i, v in enumerate(dev)])
        jumps.append([b - a for a, b in zip(*ends)])

    def first(k, carry):
        for part in range(4):
            at = pl.multiple_of(32 * k + 8 * part, 8)
            t = [c.green[q, pl.ds(at, 8), :] for q in range(9)]
            real, imag = c.chi[pl.ds(at, 8), :128], c.chi[pl.ds(at, 8), 128:]
            one, two = green(jumps[0], t[:6], t[6:]), green(jumps[1], t[:6], t[6:])
            for q in range(6):
                rows = slice(32 * q + 8 * part, 32 * q + 8 * part + 8)
                c.spec[rows, :128] = real * one[q] - imag * two[q]
                c.spec[rows, 128:] = real * two[q] + imag * one[q]
        back_right(c, k)
        return carry

    lax.fori_loop(0, 8, first, 0)
    left(c, c.li_h, c.li_l, c.u)

    def stress(r, carry):
        at = pl.multiple_of(16 * r, 16)
        kappa, shear, scale = materials(c.phase[pl.ds(at, 16), :] == 1)
        for q in range(2):
            rows = pl.ds(pl.multiple_of(256 * q + 16 * r, 16), 16)
            field = [
                jnp.concatenate([e[q][i]] * 2, axis=0) - c.u[rows, pl.ds(128 * i, 128)]
                for i in range(6)
            ]
            kt, dev, stiff, _ = law(field, kappa, shear, scale)
            for i in range(6):
                c.f[rows, pl.ds(128 * i, 128)] = field[i]
                high, low = split(stiff * dev[i] + (kt if i < 3 else 0.0))
                c.x_h[rows, pl.ds(128 * i, 128)] = high
                c.x_l[rows, pl.ds(128 * i, 128)] = low
        return carry

    lax.fori_loop(0, 16, stress, 0)
    left(c, c.lf_h, c.lf_l, c.u)

    def middle(k, carry):
        near, far = pl.multiple_of(32 * k, 32), pl.multiple_of(256 + 32 * k, 32)
        rows = jnp.concatenate(
            [
                jnp.concatenate(
                    [c.u[pl.ds(near, 32), pl.ds(128 * q, 128)], c.u[pl.ds(far, 32), pl.ds(128 * q, 128)]],
                    axis=1,
                )
                for q in range(6)
            ],
            axis=0,
        )
        high, low = split(rows)
        c.spec[...] = dot3(high, low, c.rf_h[k], c.rf_l[k])
        for part in range(4):
            at = pl.multiple_of(32 * k + 8 * part, 8)
            t = [c.green[q, pl.ds(at, 8), :] for q in range(9)]
            for half in range(2):
                cols = slice(128 * half, 128 * half + 128)
                spots = [slice(32 * q + 8 * part, 32 * q + 8 * part + 8) for q in range(6)]
                out = green([c.spec[s, cols] for s in spots], t[:6], t[6:])
                for s, v in zip(spots, out):
                    c.spec[s, cols] = v
        back_right(c, k)
        return carry

    lax.fori_loop(0, 8, middle, 0)
    left(c, c.li_h, c.li_l, c.u)

    for q in range(2):
        keep = jnp.broadcast_to((turns[q] > 1.5).astype(F32), (8, 128))

        def total(r, sums, q=q, keep=keep):
            at = pl.multiple_of(8 * r, 8)
            kappa, shear, scale = materials(c.phase[pl.ds(at, 8), :] == 1)
            rows = pl.ds(pl.multiple_of(256 * q + 8 * r, 8), 8)
            field = [
                c.f[rows, pl.ds(128 * i, 128)] - keep * c.u[rows, pl.ds(128 * i, 128)]
                for i in range(6)
            ]
            kt, dev, stiff, factor = law(field, kappa, shear, scale)
            weight = stiff * factor * factor * scale
            heavy = [weight * v for v in dev]
            new = [kt] + [stiff * v for v in dev] + [shear * factor]
            new += [heavy[i] * dev[j] for i, j in UPPER] + [kappa]
            return tuple(s + v for s, v in zip(sums, new))

        sums = lax.fori_loop(0, 32, total, (jnp.zeros((8, 128), F32),) * 30)
        for n, v in enumerate(sums):
            c.sums[pl.ds(256 * q + 8 * n, 8), :] = v
        c.sums[pl.ds(256 * q + 240, 16), :] = jnp.zeros((16, 128), F32)
    ones = jnp.ones((8, 128), F32)
    lanes = lax.dot_general(
        ones, c.sums[...], (((1,), (1,)), ((), ())), precision=EXACT, preferred_element_type=F32
    )
    return exact_dot(lanes, c.summary[...])


def finish(c, listed, out_ref):
    dev, grp = lax.axis_index("dev"), lax.axis_index("grp")
    sub, lane = iota((8, 128), 0), iota((8, 128), 1)
    step = jnp.where(sub < 2, 0, jnp.where(sub < 4, -1, 1))
    point = (2 * (jnp.full((8, 128), dev, jnp.int32) + step) + sub % 2).astype(F32)
    point = jnp.where(sub < 6, point, NONE)
    found, masked = point_rows(c.rows[...], point, 1, c.small[:, 1024:1280])
    direction = exact_dot(masked, c.small[:, 1280:1408])
    index = iota((8, 256), 1).astype(F32)
    wide = jnp.concatenate([point, point], axis=1)
    owners = jnp.broadcast_to(c.owner[...].astype(F32), (8, 256))
    who = jnp.sum(jnp.where(index == wide, owners, 0.0), axis=1, keepdims=True)
    rank = jnp.sum(
        jnp.where((owners == who) & (index < wide), 1.0, 0.0), axis=1, keepdims=True
    )
    slot = jnp.floor(rank * 0.5)
    core = jnp.full((8, 1), grp, jnp.int32).astype(F32)
    ours = (rank - 2.0 * slot) == core
    pick = ((lanes_f32() == who) & ours).astype(F32)

    gather_wait(c.results, c.send_b, c.recv_b)
    value = exact_dot(pick, c.results[...])
    value = jnp.where(slot > 0.5, pltpu.roll(value, 64, 1), value)
    value = jnp.where(lane < 64, value, 0.0)
    c.swap[0] = value
    copy = pltpu.make_async_remote_copy(
        src_ref=c.swap.at[0], dst_ref=c.swap.at[1], send_sem=c.send_c, recv_sem=c.recv_c,
        device_id=sibling(), device_id_type=MESH,
    )
    copy.start()
    copy.wait()
    value = value + c.swap[1]
    out_ref[0] = value
    terms = value * jnp.where(lane < 6, 1.0, direction)
    dealt = exact_dot(terms, c.small[:, 1408:1664])
    own_lane = lane % 2 == sub % 2
    twelve = lane % 16 < 12
    for half in range(2):
        y = jnp.where(own_lane, dealt[:, 128 * half : 128 * half + 128], 0.0)
        mine = jnp.sum(jnp.where(sub < 2, y, 0.0), axis=0, keepdims=True)
        linked = y * found
        before = jnp.sum(jnp.where((sub == 2) | (sub == 3), linked, 0.0), axis=0, keepdims=True)
        after = jnp.sum(jnp.where((sub == 4) | (sub == 5), linked, 0.0), axis=0, keepdims=True)
        out = jnp.zeros((8, 128), F32)
        for n in range(4):
            got = jnp.sum(c.near[n] * jnp.where(lane < 12, mine, 0.0), axis=1, keepdims=True)
            out = jnp.where(lane == n, got, out)
        for end, row, lead in ((0, before, 5), (1, after, 2)):
            part = jnp.where(twelve & (lane // 16 == sub + lead) & (sub < 3), row, 0.0)
            got = jnp.sum(part, axis=1, keepdims=True)
            out = out + jnp.where(lane == listed[end], got, 0.0)
        out_ref[1 + half] = out


TABLES = {
    "lf": ((2, 512, 512), BF16),
    "rf": ((2, 8, 256, 256), BF16),
    "li": ((2, 512, 512), BF16),
    "ri": ((2, 8, 256, 256), BF16),
    "green": ((9, 256, 128), F32),
    "small": ((128, 1664), F32),
    "summary": ((512, 128), F32),
    "phase": ((256, 128), jnp.int32),
}
WORK = {
    "chi": ((256, 256), F32),
    "spec": ((192, 256), F32),
    "x_h": ((512, 768), BF16),
    "x_l": ((512, 768), BF16),
    "u": ((512, 768), F32),
    "f": ((512, 768), F32),
    "sums": ((512, 128), F32),
    "flat": ((128, 128), F32),
    "near": ((4, 8, 128), F32),
    "note": ((8, 128), F32),
    "rows": ((128, 128), F32),
    "results": ((128, 128), F32),
    "swap": ((2, 8, 128), F32),
}
SEMS = ("send", "recv", "send_b", "recv_b", "send_c", "recv_c")
INPUTS = ("disp", "probe", "b", "conn", "listed", "owner", "counts")


class Bag:
    def __init__(self, **refs):
        self.__dict__.update(refs)


def constants():
    out = dict(zip(("lf", "rf", "li", "ri"), (np.stack(two_parts(t)) for t in dft_tables())))
    spread_u, splat, spread_v, expand, deal = message_tables()
    out["small"] = np.concatenate([spread_u, splat, spread_v, expand, deal], axis=1)
    out["green"], out["summary"] = green_tables(), summary_table()
    return out


def splats(c, point):
    _, masked = point_rows(c.rows[...], point, 0, c.small[:, :256])
    strain = exact_dot(masked, c.small[:, 256:1024])
    return [
        [jnp.broadcast_to(strain[q : q + 1, 128 * i : 128 * i + 128], (8, 128)) for i in range(6)]
        for q in range(2)
    ]


def main_kernel(*refs):
    names = INPUTS + tuple(k + "_in" for k in TABLES) + ("out",) + tuple(TABLES) + tuple(WORK)
    c = Bag(**dict(zip(names + SEMS + ("loads",), refs)))
    loads = {
        k: pltpu.make_async_copy(getattr(c, k + "_in"), getattr(c, k), c.loads.at[n])
        for n, k in enumerate(TABLES)
    }
    for k in ("phase", "lf", "rf", "small", "li", "ri", "green", "summary"):
        loads[k].start()
    barrier = greet()
    row = partition_row(c.disp, c.probe, c.b, c.conn, c.listed, c.flat, c.near)
    c.note[...] = jnp.broadcast_to(row, (8, 128))
    pl.semaphore_wait(barrier, 128)
    gather_start(c.note, c.rows, c.send, c.recv)
    for k in TABLES:
        loads[k].wait()
    c.lf_h, c.lf_l, c.li_h, c.li_l = c.lf.at[0], c.lf.at[1], c.li.at[0], c.li.at[1]
    c.rf_h, c.rf_l, c.ri_h, c.ri_l = c.rf.at[0], c.rf.at[1], c.ri.at[0], c.ri.at[1]
    phase_spectrum(c)
    point, turns = my_points(c.owner[...], c.counts[...])
    gather_wait(c.rows, c.send, c.recv)
    c.note[...] = solve(c, splats(c, point), turns)
    gather_start(c.note, c.results, c.send_b, c.recv_b)
    finish(c, c.listed, c.out)


def last_kernel(packed, stress, force, image):
    stress[...] = packed[0, :2, :6]
    force[...] = packed[1, :3, :4]
    image[...] = packed[2, :3, :4]


VM = pl.BlockSpec(memory_space=pltpu.VMEM)
SM = pl.BlockSpec(memory_space=pltpu.SMEM)
FAR_OFF = pl.BlockSpec(memory_space=pltpu.HBM)


def on_device(disp, probe, strain_disp, conn, halo_rows, owner, counts, phase):
    table = {k: jnp.asarray(v) for k, v in constants().items()}
    table["phase"] = phase.reshape(256, 128)
    shape = jax.ShapeDtypeStruct
    packed = pl.pallas_call(
        main_kernel,
        out_shape=shape((3, 8, 128), F32),
        in_specs=[SM, SM, VM, VM, SM, VM, VM] + [FAR_OFF] * len(TABLES),
        out_specs=VM,
        scratch_shapes=[pltpu.VMEM(*v) for v in TABLES.values()]
        + [pltpu.VMEM(*v) for v in WORK.values()]
        + [pltpu.SemaphoreType.DMA] * len(SEMS)
        + [pltpu.SemaphoreType.DMA((8,))],
        compiler_params=pltpu.CompilerParams(
            collective_id=0, has_side_effects=True, vmem_limit_bytes=48 << 20
        ),
    )(
        disp, probe, strain_disp.transpose(0, 2, 1), conn.T, halo_rows,
        owner.reshape(1, 256), counts.reshape(1, 256), *[table[k] for k in TABLES],
    )
    stress, force, image = pl.pallas_call(
        last_kernel,
        out_shape=(shape((2, 6), F32), shape((3, 4), F32), shape((3, 4), F32)),
        in_specs=[VM],
        out_specs=(VM, VM, VM),
    )(packed)
    return stress.T, force, image


def solution(mesh):
    dev = P(None, "dev")
    return jax.shard_map(
        on_device,
        mesh=mesh,
        in_specs=(dev, dev, P(None, None, "dev"), dev, P("dev"), P(), P(), P("dev", None)),
        out_specs=(dev, dev, dev),
        check_vma=False,
    )
```

```python
import jax
import jax.numpy as jnp
import ml_dtypes
import numpy as np
from jax import lax
from jax.experimental import pallas as pl
from jax.experimental.pallas import tpu as pltpu
from jax.sharding import PartitionSpec as P

EXACT = lax.Precision.HIGHEST
F32 = jnp.float32
BF16 = jnp.bfloat16
MESH = pl.DeviceIdType.MESH
VOXELS = 32768
ROOT_TWO = 1.4142135623730951
KAPPA = (2.0, 2.4)
SHEAR = (1.0, 1.3)
SOFT = (0.4, 2.5)
KAPPA_MEDIUM = 2.2
SHEAR_MEDIUM = 0.75
LAME_MEDIUM = KAPPA_MEDIUM - 2.0 * SHEAR_MEDIUM / 3.0
COUPLING = (LAME_MEDIUM + SHEAR_MEDIUM) / (LAME_MEDIUM + 2.0 * SHEAR_MEDIUM)
UPPER = [(i, j) for i in range(6) for j in range(i, 6)]
NONE = 4096.0


def two_parts(table):
    high = table.astype(np.float32).astype(ml_dtypes.bfloat16)
    low = (table - high.astype(np.float64)).astype(np.float32).astype(ml_dtypes.bfloat16)
    return high, low


def dft_tables():
    n32, n16, n8, n4 = np.arange(32), np.arange(16), np.arange(8), np.arange(4)
    f32 = np.exp(-2j * np.pi / 32 * np.outer(n32, n32))
    f8 = np.exp(-2j * np.pi / 8 * np.outer(n8, n8))
    f4 = np.exp(-2j * np.pi / 4 * np.outer(n4, n4))
    lefts, rights = [], []
    for odd in range(2):
        half = np.exp(-2j * np.pi / 32 * np.outer(2 * n16 + odd, n16))
        one = np.einsum("ab,cd->cabd", half, f8).reshape(128, 128)
        lefts.append(np.block([[one.real, -one.imag], [one.imag, one.real]]))
    for k0 in range(8):
        turn = np.exp(-2j * np.pi / 32 * n4 * k0)[:, None] * f4
        one = np.einsum("ab,cd->acbd", turn, f32).reshape(128, 128)
        rights.append(np.block([[one.real, one.imag], [-one.imag, one.real]]))
    left, right = np.stack(lefts), np.stack(rights)
    return left, right, left.transpose(0, 2, 1) / VOXELS, right.transpose(0, 2, 1)


def green_tables():
    row, lane = np.arange(256)[:, None], np.arange(128)[None, :]
    k = [2 * (row % 16) + row % 32 // 16 + 0 * lane, 8 * (lane // 32) + row // 32, lane % 32 + 0 * row]
    freq = [np.where(v < 16, v, v - 32).astype(np.float64) for v in k]
    length = np.sqrt(np.maximum(sum(f * f for f in freq), 1.0))
    normal = [f / length for f in freq]
    edge = [v == 16 for v in k]
    pairs = [(0, 0), (1, 1), (2, 2), (1, 2), (0, 2), (0, 1)]
    both = [
        normal[i] * normal[j] * (1.0 if i == j else ROOT_TWO) / SHEAR_MEDIUM for i, j in pairs
    ]
    even = [np.where(edge[i] == edge[j], v, 0.0) for (i, j), v in zip(pairs, both)]
    odd = [np.where(edge[i] == edge[j], 0.0, v) for (i, j), v in zip(pairs, both)][3:]
    return np.stack(even + odd).astype(np.float32)


def message_tables():
    spread = np.zeros((2, 2, 128, 128), np.float32)
    for uv in range(2):
        for d in range(3):
            for j in range(12):
                spread[uv, 0, 16 * d + 12 + uv, 32 + 16 * d + j] = 1.0
                spread[uv, 1, 16 * d + 14 + uv, 80 + 16 * d + j] = 1.0
    splat = np.zeros((128, 6, 128), np.float32)
    expand = np.zeros((128, 128), np.float32)
    weigh = np.zeros((128, 2, 128), np.float32)
    for g in range(8):
        for i in range(6):
            for p in range(2):
                splat[16 * g + 2 * i + p, i, :] = 1.0
                weigh[16 * g + 2 * i + p, p, i] = 1.0
                for k in range(6):
                    expand[16 * g + 2 * i + p, 8 + 6 * i + k] = 1.0
                    weigh[16 * g + 2 * i + p, p, 8 + 6 * k + i] = 1.0
    pack = lambda a: a.transpose(1, 0, 2).reshape(128, -1)
    flat = lambda a: a.reshape(128, -1)
    return pack(spread[0]), flat(splat), pack(spread[1]), expand, flat(weigh)


def summary_table():
    table = np.zeros((2, 32, 8, 128), np.float64)
    unit = np.array([1.0, 1, 1, 0, 0, 0])
    outer = np.outer(unit, unit)
    project = np.eye(6) - outer / 3.0
    for q in range(2):
        for i in range(6):
            table[q, 0, :, 64 * q + i] = unit[i]
            table[q, 1 + i, :, 64 * q + i] = 1.0
            for j in range(6):
                lane = 64 * q + 8 + 6 * j + i
                table[q, 29, :, lane] = outer[i, j]
                table[q, 7, :, lane] = 2.0 * project[i, j]
                place = UPPER.index((min(i, j), max(i, j)))
                table[q, 8 + place, :, lane] = -1.0
    return table.reshape(512, 128) / VOXELS


def iota(shape, dim):
    return lax.broadcasted_iota(jnp.int32, shape, dim)


def lanes_f32():
    return iota((8, 128), 1).astype(F32)


def two_dot(a, b):
    high, low = split(a)
    out = jnp.dot(jnp.concatenate([high, low], axis=0), b, preferred_element_type=F32)
    return out[: a.shape[0]] + out[a.shape[0] :]


def split(value):
    high = value.astype(BF16)
    return high, (value - high.astype(F32)).astype(BF16)


def dot3(a_high, a_low, b_high, b_low):
    out = jnp.dot(a_high, b_high, preferred_element_type=F32)
    out = out + jnp.dot(a_low, b_high, preferred_element_type=F32)
    return out + jnp.dot(a_high, b_low, preferred_element_type=F32)


FAR = (4, 5, 3, 6, 2, 7, 1, 0)


def each_peer(action):
    dev = lax.axis_index("dev")
    for across in FAR:
        level = (dev // 16 + across) % 8

        def one(j, carry, level=level):
            action(level * 16 + (dev + j) % 16)
            return carry

        lax.fori_loop(1 if across == 0 else 0, 16, one, 0)


def sibling():
    return ((lax.axis_index("grp") + 1) % 2, lax.axis_index("dev"))


def greet():
    barrier = pltpu.get_barrier_semaphore()
    grp = lax.axis_index("grp")

    def signal(peer):
        pl.semaphore_signal(barrier, inc=1, device_id=peer, device_id_type=MESH)

    each_peer(lambda dev: signal((grp, dev)))
    signal(sibling())
    return barrier


def gather_start(note, rows, send, recv):
    dev, grp = lax.axis_index("dev"), lax.axis_index("grp")
    src, dst = note.at[pl.ds(0, 1)], rows.at[pl.ds(dev, 1)]

    def start(peer):
        pltpu.make_async_remote_copy(
            src_ref=src, dst_ref=dst, send_sem=send, recv_sem=recv,
            device_id=(grp, peer), device_id_type=MESH,
        ).start()

    each_peer(start)
    pltpu.make_async_copy(src, dst, recv).start()


def gather_wait(rows, send, recv):
    pltpu.make_async_copy(rows, rows, recv).wait()
    most = rows.at[pl.ds(0, 127)]
    pltpu.make_async_copy(most, most, send).wait()


def partition_row(disp, probe, b_ref, conn_ref, listed, flat, near_ref):
    lane, sub = iota((8, 128), 1), iota((8, 128), 0)
    flat[...] = jnp.zeros((128, 128), F32)
    for i in range(6):
        flat[pl.ds(2 * i, 2), pl.ds(0, 24)] = b_ref[i]
    axis = lane % 3
    spread = (lane // 3 == sub).astype(F32)
    conn = jnp.dot(conn_ref[...].astype(F32), spread, preferred_element_type=F32)
    values = []
    for field in (disp, probe):
        values.append(
            [
                jnp.where(axis == 0, field[0, n], jnp.where(axis == 1, field[1, n], field[2, n]))
                for n in range(4)
            ]
        )
    blocks, nears = [], []
    for p in range(2):
        c = jnp.broadcast_to(conn[p : p + 1], (8, 128))
        block = ((c == 4.0) & (axis == sub - 2)) | ((c == 5.0) & (axis == sub - 5))
        block = block.astype(F32)
        for uv in range(2):
            value = jnp.zeros((8, 128), F32)
            for n in range(4):
                value = jnp.where(c == float(n), values[uv][n], value)
            block = jnp.where(sub == uv, value, block)
        blocks.append(block)
        nears.append([((c == float(n)) & (axis == sub)).astype(F32) for n in range(4)])
    heap = blocks + [nears[p][n] for n in range(4) for p in range(2)]
    w = lax.dot_general(
        jnp.concatenate(heap, axis=0), flat[...], (((1,), (1,)), ((), ())),
        precision=EXACT, preferred_element_type=F32,
    )
    even = lane % 2 == 0
    x = jnp.where(even, w[:8], w[8:16])
    total = jnp.where(sub == 0, x, 0.0)
    for g in range(1, 8):
        total = total + pltpu.roll(jnp.where(sub == g, x, 0.0), 16 * g, 1)
    row = jnp.sum(total, axis=0, keepdims=True)
    for n in range(4):
        at = 16 + 16 * n
        near_ref[n] = jnp.where(even, w[at : at + 8], w[at + 8 : at + 16])
    for way in range(2):
        want = jnp.full((1, 128), listed[1 - way], jnp.int32)
        for uv in range(2):
            sent = jnp.zeros((1, 128), F32)
            for n in range(4):
                field = (disp, probe)[uv]
                third = lane[:1] // 16
                value = jnp.where(
                    third == 0, field[0, n], jnp.where(third == 1, field[1, n], field[2, n])
                )
                sent = jnp.where(want == n, value, sent)
            place = (lane[:1] < 48) & (lane[:1] % 16 == 12 + 2 * way + uv)
            row = jnp.where(place, sent, row)
    return row


def point_rows(rows, point, uv, spread):
    lane = lanes_f32()
    part = jnp.floor(point * 0.5)
    parity = point - 2.0 * part
    pick = jnp.concatenate([lane == part, lane == part - 1.0, lane == part + 1.0], axis=0)
    both = jnp.dot(
        pick.astype(F32).astype(BF16), jnp.concatenate(split(rows), axis=1),
        preferred_element_type=F32,
    )
    found = both[:, :128] + both[:, 128:]
    met = two_dot(found[8:], spread)
    below, above = met[:8, :128], met[8:, 128:]
    count = iota((8, 128), 1)
    base = ((count // 16) == uv).astype(F32)
    own = (count % 2).astype(F32) == parity
    factor = jnp.where((count % 16) < 12, base + below + above, 0.0)
    return found[:8], jnp.where(own, found[:8] * factor, 0.0)


def my_points(owner, counts):
    me, grp = lax.axis_index("dev"), lax.axis_index("grp")
    index = iota((1, 256), 1).astype(F32)
    mine = owner == me
    first = jnp.min(jnp.where(mine, index, NONE), axis=1, keepdims=True)
    second = jnp.min(jnp.where(mine & (index > first), index, NONE), axis=1, keepdims=True)
    third = jnp.min(jnp.where(mine & (index > second), index, NONE), axis=1, keepdims=True)
    even = jnp.full((1, 1), grp, jnp.int32) == 0
    slots = (jnp.where(even, first, second), jnp.where(even, third, NONE))
    sub = iota((8, 128), 0)
    point = jnp.where(sub == 0, slots[0], jnp.where(sub == 1, slots[1], NONE))
    turns = [
        jnp.sum(jnp.where(index == slot, counts.astype(F32), 0.0), axis=1, keepdims=True)
        for slot in slots
    ]
    return point, turns


def green(tau, t, odd):
    half = [0.5 * t[q] for q in (3, 4, 5)]
    cross = [v * (1.0 / ROOT_TWO) for v in half]
    p3, p4, p5 = (half[0] * tau[3], half[1] * tau[4], half[2] * tau[5])
    d0, d1, d2 = (t[0] * tau[0], t[1] * tau[1], t[2] * tau[2])
    along = (COUPLING * SHEAR_MEDIUM) * (d0 + d1 + d2 + 2.0 * (p3 + p4 + p5))
    aside = (COUPLING * SHEAR_MEDIUM) * (odd[0] * tau[3] + odd[1] * tau[4] + odd[2] * tau[5])
    s12, s02, s01 = (0.5 * (t[1] + t[2]), 0.5 * (t[0] + t[2]), 0.5 * (t[0] + t[1]))
    return [
        d0 + p5 + p4 - along * t[0],
        d1 + p5 + p3 - along * t[1],
        d2 + p4 + p3 - along * t[2],
        cross[2] * tau[4] + cross[1] * tau[5] + half[0] * (tau[1] + tau[2]) + s12 * tau[3]
        - along * t[3] - aside * odd[0],
        cross[2] * tau[3] + cross[0] * tau[5] + half[1] * (tau[0] + tau[2]) + s02 * tau[4]
        - along * t[4] - aside * odd[1],
        cross[1] * tau[3] + cross[0] * tau[4] + half[2] * (tau[0] + tau[1]) + s01 * tau[5]
        - along * t[5] - aside * odd[2],
    ]


def law(e, kappa, shear, scale):
    trace = e[0] + e[1] + e[2]
    third = trace * (1.0 / 3.0)
    dev = [e[i] - third for i in range(3)] + list(e[3:])
    size = dev[0] * dev[0]
    for v in dev[1:]:
        size = size + v * v
    factor = lax.rsqrt(1.0 + size * scale)
    return kappa * trace, dev, 2.0 * shear * factor, factor


def by_phase(hard, pair):
    return jnp.where(hard, pair[1], pair[0])


def materials(hard):
    return (
        by_phase(hard, KAPPA), by_phase(hard, SHEAR),
        by_phase(hard, (1.0 / SOFT[0] ** 2, 1.0 / SOFT[1] ** 2)),
    )


def phase_spectrum(c):
    pattern = (c.phase[...] == 1).astype(F32)
    halves = (pattern[:128] + pattern[128:], pattern[:128] - pattern[128:])
    z = []
    for odd in range(2):
        half = halves[odd].astype(BF16)
        one = jnp.dot(c.lf_h[odd, :, :128], half, preferred_element_type=F32)
        z.append(one + jnp.dot(c.lf_l[odd, :, :128], half, preferred_element_type=F32))
    for k in range(8):
        rows = jnp.concatenate(
            [
                jnp.concatenate([v[16 * k : 16 * k + 16], v[128 + 16 * k : 144 + 16 * k]], axis=1)
                for v in z
            ],
            axis=0,
        )
        high, low = split(rows)
        c.chi[32 * k : 32 * k + 32, :] = dot3(high, low, c.rf_h[k], c.rf_l[k])


def back_right(c, k):
    high, low = split(c.spec[k])
    w = dot3(high, low, c.ri_h[k], c.ri_l[k])
    high, low = split(w)
    for q in range(6):
        for odd in range(2):
            for part in range(2):
                at = 256 * odd + 128 * part + 16 * k
                at = (slice(at, at + 16), slice(128 * q, 128 * q + 128))
                lead = 32 * q + 16 * odd
                from_ = (slice(lead, lead + 16), slice(128 * part, 128 * part + 128))
                c.x_h[at] = high[from_]
                c.x_l[at] = low[from_]


def left(c, high, low, out):
    for odd in range(2):
        rows = slice(256 * odd, 256 * odd + 256)
        for q in range(3):
            cols = slice(256 * q, 256 * q + 256)
            out[rows, cols] = dot3(high[odd], low[odd], c.x_h[rows, cols], c.x_l[rows, cols])


def solve(c, e, turns):
    jumps = []
    for q in range(2):
        ends = []
        for m in range(2):
            kt, dev, stiff, _ = law(e[q], KAPPA[m], SHEAR[m], 1.0 / SOFT[m] ** 2)
            ends.append([stiff * v + (kt if i < 3 else 0.0) for i, v in enumerate(dev)])
        jumps.append([b - a for a, b in zip(*ends)])

    for k in range(8):
        for part in range(4):
            at = 32 * k + 8 * part
            t = [c.green[q, at : at + 8, :] for q in range(9)]
            real, imag = c.chi[at : at + 8, :128], c.chi[at : at + 8, 128:]
            one, two = green(jumps[0], t[:6], t[6:]), green(jumps[1], t[:6], t[6:])
            for q in range(6):
                rows = slice(32 * q + 8 * part, 32 * q + 8 * part + 8)
                c.spec[k, rows, :128] = real * one[q] - imag * two[q]
                c.spec[k, rows, 128:] = real * two[q] + imag * one[q]
        back_right(c, k)
    left(c, c.li_h, c.li_l, c.u)

    def halves(ref, lead, r, step):
        near, far = (pl.ds(pl.multiple_of(at + lead + step * r, step), step) for at in (0, 256))
        cols = [pl.ds(128 * i, 128) for i in range(6)]
        even, odd = [ref[near, v] for v in cols], [ref[far, v] for v in cols]
        return [a + b for a, b in zip(even, odd)], [a - b for a, b in zip(even, odd)]

    def stress(r, carry):
        for q in range(2):
            sides = []
            for side, moved in enumerate(halves(c.u, 128 * q, r, 16)):
                at = pl.ds(pl.multiple_of(128 * side + 16 * r, 16), 16)
                kappa, shear, scale = materials(c.phase[at, :] == 1)
                field = [jnp.concatenate([e[q][i]] * 2, axis=0) - moved[i] for i in range(6)]
                kt, dev, stiff, _ = law(field, kappa, shear, scale)
                rows = pl.ds(pl.multiple_of(256 * side + 128 * q + 16 * r, 16), 16)
                for i in range(6):
                    c.f[rows, pl.ds(128 * i, 128)] = field[i]
                sides.append([stiff * dev[i] + (kt if i < 3 else 0.0) for i in range(6)])
            for i in range(6):
                for odd in range(2):
                    a, b = sides[0][i], sides[1][i]
                    high, low = split(a - b if odd else a + b)
                    rows = pl.ds(pl.multiple_of(256 * odd + 128 * q + 16 * r, 16), 16)
                    c.x_h[rows, pl.ds(128 * i, 128)] = high
                    c.x_l[rows, pl.ds(128 * i, 128)] = low
        return carry

    lax.fori_loop(0, 8, stress, 0)
    left(c, c.lf_h, c.lf_l, c.u)

    for k in range(8):
        rows = []
        for q in range(6):
            cols = slice(128 * q, 128 * q + 128)
            for odd in range(2):
                at = 256 * odd + 16 * k
                pair = [c.u[at : at + 16, cols], c.u[128 + at : 144 + at, cols]]
                rows.append(jnp.concatenate(pair, axis=1))
        high, low = split(jnp.concatenate(rows, axis=0))
        c.spec[k] = dot3(high, low, c.rf_h[k], c.rf_l[k])
        for part in range(4):
            at = 32 * k + 8 * part
            t = [c.green[q, at : at + 8, :] for q in range(9)]
            for half in range(2):
                cols = slice(128 * half, 128 * half + 128)
                spots = [slice(32 * q + 8 * part, 32 * q + 8 * part + 8) for q in range(6)]
                out = green([c.spec[k, v, cols] for v in spots], t[:6], t[6:])
                for v, new in zip(spots, out):
                    c.spec[k, v, cols] = new
        back_right(c, k)
    left(c, c.li_h, c.li_l, c.u)

    for q in range(2):
        keep = jnp.broadcast_to((turns[q] > 1.5).astype(F32), (8, 128))

        def total(r, sums, q=q, keep=keep):
            for side, moved in enumerate(halves(c.u, 128 * q, r, 8)):
                at = pl.ds(pl.multiple_of(128 * side + 8 * r, 8), 8)
                kappa, shear, scale = materials(c.phase[at, :] == 1)
                rows = pl.ds(pl.multiple_of(256 * side + 128 * q + 8 * r, 8), 8)
                field = [c.f[rows, pl.ds(128 * i, 128)] - keep * moved[i] for i in range(6)]
                kt, dev, stiff, factor = law(field, kappa, shear, scale)
                weight = stiff * factor * factor * scale
                heavy = [weight * v for v in dev]
                new = [kt] + [stiff * v for v in dev] + [shear * factor]
                new += [heavy[i] * dev[j] for i, j in UPPER] + [kappa]
                sums = tuple(s + v for s, v in zip(sums, new))
            return sums

        sums = lax.fori_loop(0, 16, total, (jnp.zeros((8, 128), F32),) * 30)
        for n, v in enumerate(sums):
            c.sums[256 * q + 8 * n : 256 * q + 8 * n + 8, :] = v
        c.sums[256 * q + 240 : 256 * q + 256, :] = jnp.zeros((16, 128), F32)
    ones = jnp.ones((8, 128), BF16)
    across = (((1,), (1,)), ((), ()))
    lanes = [
        lax.dot_general(ones, v, across, preferred_element_type=F32) for v in split(c.sums[...])
    ]
    high, low = split(lanes[0] + lanes[1])
    out = jnp.dot(jnp.concatenate([high, low]), c.summary[0], preferred_element_type=F32)
    return out[:8] + out[8:] + jnp.dot(high, c.summary[1], preferred_element_type=F32)


def finish(c, listed, out_ref):
    dev, grp = lax.axis_index("dev"), lax.axis_index("grp")
    sub, lane = iota((8, 128), 0), iota((8, 128), 1)
    step = jnp.where(sub < 2, 0, jnp.where(sub < 4, -1, 1))
    point = (2 * (jnp.full((8, 128), dev, jnp.int32) + step) + sub % 2).astype(F32)
    point = jnp.where(sub < 6, point, NONE)
    found, masked = point_rows(c.rows[...], point, 1, c.small[:, 1024:1280])
    factor = jnp.where(lane < 6, 1.0, two_dot(masked, c.small[:, 1280:1408]))
    linked = [
        jnp.where((lane // 16 == sub + lead) & (sub < 3), found[at : at + 1], 0.0)
        for at, lead in ((2, 5), (4, 2))
    ]
    parts = jnp.concatenate([c.near[n] for n in range(4)] + linked, axis=0)
    spread = two_dot(parts, c.small[:, 1408:1664])
    weights = []
    for n in range(6):
        first = 2 * max(0, n - 3)
        weights.append(
            [
                spread[8 * n : 8 * n + 8, 128 * p : 128 * p + 128] * factor[first + p : first + p + 1]
                for p in range(2)
            ]
        )
    index = iota((8, 256), 1).astype(F32)
    wide = jnp.concatenate([point, point], axis=1)
    owners = jnp.broadcast_to(c.owner[...].astype(F32), (8, 256))
    who = jnp.sum(jnp.where(index == wide, owners, 0.0), axis=1, keepdims=True)
    rank = jnp.sum(
        jnp.where((owners == who) & (index < wide), 1.0, 0.0), axis=1, keepdims=True
    )
    slot = jnp.floor(rank * 0.5)
    core = jnp.full((8, 1), grp, jnp.int32).astype(F32)
    place = jnp.where((rank - 2.0 * slot) == core, who, NONE)
    row = iota((128, 128), 0).astype(F32)

    gather_wait(c.results, c.send_b, c.recv_b)
    results = c.results[...]
    value = jnp.zeros((8, 128), F32)
    for q in range(6):
        one = jnp.sum(jnp.where(row == place[q : q + 1], results, 0.0), axis=0, keepdims=True)
        value = jnp.where(sub == q, one, value)
    value = jnp.where(slot > 0.5, pltpu.roll(value, 64, 1), value)
    value = jnp.where(lane < 64, value, 0.0)
    c.swap[0] = value
    copy = pltpu.make_async_remote_copy(
        src_ref=c.swap.at[0], dst_ref=c.swap.at[1], send_sem=c.send_c, recv_sem=c.recv_c,
        device_id=sibling(), device_id_type=MESH,
    )
    copy.start()
    copy.wait()
    value = value + c.swap[1]
    out_ref[0] = value
    sums = []
    for n in range(6):
        first = 2 * max(0, n - 3)
        a, b = weights[n]
        sums.append(a * value[first : first + 1] + b * value[first + 1 : first + 2])
    for half in range(2):
        out = jnp.zeros((8, 128), F32)
        mine = (lane >= 8) if half else (lane < 8)
        for n in range(6):
            got = jnp.sum(jnp.where(mine, sums[n], 0.0), axis=1, keepdims=True)
            if n < 4:
                out = jnp.where(lane == n, got, out)
            else:
                out = out + jnp.where(lane == listed[n - 4], got, 0.0)
        out_ref[1 + half] = out


TABLES = {
    "lf": ((2, 2, 256, 256), BF16),
    "rf": ((2, 8, 256, 256), BF16),
    "li": ((2, 2, 256, 256), BF16),
    "ri": ((2, 8, 256, 256), BF16),
    "green": ((9, 256, 128), F32),
    "small": ((128, 1664), BF16),
    "summary": ((2, 512, 128), BF16),
    "phase": ((256, 128), jnp.int32),
}
WORK = {
    "chi": ((256, 256), F32),
    "spec": ((8, 192, 256), F32),
    "x_h": ((512, 768), BF16),
    "x_l": ((512, 768), BF16),
    "u": ((512, 768), F32),
    "f": ((512, 768), F32),
    "sums": ((512, 128), F32),
    "flat": ((128, 128), F32),
    "near": ((4, 8, 128), F32),
    "note": ((8, 128), F32),
    "rows": ((128, 128), F32),
    "results": ((128, 128), F32),
    "swap": ((2, 8, 128), F32),
}
SEMS = ("send", "recv", "send_b", "recv_b", "send_c", "recv_c")
INPUTS = ("disp", "probe", "b", "conn", "listed", "owner", "counts")


class Bag:
    def __init__(self, **refs):
        self.__dict__.update(refs)


def constants():
    out = dict(zip(("lf", "rf", "li", "ri"), (np.stack(two_parts(t)) for t in dft_tables())))
    small = np.concatenate(message_tables(), axis=1)
    out["small"] = small.astype(ml_dtypes.bfloat16)
    out["green"], out["summary"] = green_tables(), np.stack(two_parts(summary_table()))
    return out


def splats(c, point):
    _, masked = point_rows(c.rows[...], point, 0, c.small[:, :256])
    strain = two_dot(masked, c.small[:, 256:1024])
    return [
        [jnp.broadcast_to(strain[q : q + 1, 128 * i : 128 * i + 128], (8, 128)) for i in range(6)]
        for q in range(2)
    ]


def main_kernel(*refs):
    names = INPUTS + tuple(k + "_in" for k in TABLES) + ("out",) + tuple(TABLES) + tuple(WORK)
    c = Bag(**dict(zip(names + SEMS + ("loads",), refs)))
    loads = {
        k: pltpu.make_async_copy(getattr(c, k + "_in"), getattr(c, k), c.loads.at[n])
        for n, k in enumerate(TABLES)
    }
    for k in ("phase", "lf", "rf", "small", "li", "ri", "green", "summary"):
        loads[k].start()
    barrier = greet()
    row = partition_row(c.disp, c.probe, c.b, c.conn, c.listed, c.flat, c.near)
    c.note[...] = jnp.broadcast_to(row, (8, 128))
    pl.semaphore_wait(barrier, 128)
    gather_start(c.note, c.rows, c.send, c.recv)
    for k in TABLES:
        loads[k].wait()
    c.lf_h, c.lf_l, c.li_h, c.li_l = c.lf.at[0], c.lf.at[1], c.li.at[0], c.li.at[1]
    c.rf_h, c.rf_l, c.ri_h, c.ri_l = c.rf.at[0], c.rf.at[1], c.ri.at[0], c.ri.at[1]
    phase_spectrum(c)
    point, turns = my_points(c.owner[...], c.counts[...])
    gather_wait(c.rows, c.send, c.recv)
    c.note[...] = solve(c, splats(c, point), turns)
    gather_start(c.note, c.results, c.send_b, c.recv_b)
    finish(c, c.listed, c.out)


def last_kernel(packed, stress, force, image):
    stress[...] = packed[0, :2, :6]
    force[...] = packed[1, :3, :4]
    image[...] = packed[2, :3, :4]


VM = pl.BlockSpec(memory_space=pltpu.VMEM)
SM = pl.BlockSpec(memory_space=pltpu.SMEM)
FAR_OFF = pl.BlockSpec(memory_space=pltpu.HBM)


def on_device(disp, probe, strain_disp, conn, halo_rows, owner, counts, phase):
    table = {k: jnp.asarray(v) for k, v in constants().items()}
    table["phase"] = phase.reshape(256, 128)
    shape = jax.ShapeDtypeStruct
    packed = pl.pallas_call(
        main_kernel,
        out_shape=shape((3, 8, 128), F32),
        in_specs=[SM, SM, VM, VM, SM, VM, VM] + [FAR_OFF] * len(TABLES),
        out_specs=VM,
        scratch_shapes=[pltpu.VMEM(*v) for v in TABLES.values()]
        + [pltpu.VMEM(*v) for v in WORK.values()]
        + [pltpu.SemaphoreType.DMA] * len(SEMS)
        + [pltpu.SemaphoreType.DMA((8,))],
        compiler_params=pltpu.CompilerParams(
            collective_id=0, has_side_effects=True, vmem_limit_bytes=63 << 20
        ),
    )(
        disp, probe, strain_disp.transpose(0, 2, 1), conn.T, halo_rows,
        owner.reshape(1, 256), counts.reshape(1, 256), *[table[k] for k in TABLES],
    )
    stress, force, image = pl.pallas_call(
        last_kernel,
        out_shape=(shape((2, 6), F32), shape((3, 4), F32), shape((3, 4), F32)),
        in_specs=[VM],
        out_specs=(VM, VM, VM),
    )(packed)
    return stress.T, force, image


def solution(mesh):
    dev = P(None, "dev")
    return jax.shard_map(
        on_device,
        mesh=mesh,
        in_specs=(dev, dev, P(None, None, "dev"), dev, P("dev"), P(), P(), P("dev", None)),
        out_specs=(dev, dev, dev),
        check_vma=False,
    )
```
